32 devices in a mesh: fsdp: 8 (over y, x, core), ctx: 4 (over z).
Axes of the slice: x: 2, y: 2, z: 4, core: 2. Of those that a mesh axis runs over, the one named last changes fastest.
Arguments:
- activations: float32 [8192, 1536], P(('fsdp', 'ctx')), may hold values from -6 to 6
- in_weight: bfloat16 [2, 1536, 6448], P(None, 'fsdp'), may hold values from -0.15625 to 0.15625
- out_weight: bfloat16 [2, 3072, 1536], P(None, 'fsdp'), may hold values from -0.109375 to 0.109375
- norm_gain: float32 [2, 1536], replicated, may hold values from 0.25 to 1.75
- conv_weight: float32 [2, 4, 3328], replicated, may hold values from -3 to 3
- conv_bias: float32 [2, 3328], replicated, may hold values from -3 to 3
- step_bias: float32 [2, 48], replicated, may hold values from -9 to -3
- decay_log: float32 [2, 48], replicated, may hold values from -1.5 to 2
- skip_gain: float32 [2, 48], replicated, may hold values from 0.5 to 1.5
- gate_gain: float32 [2, 3072], replicated, may hold values from 0.25 to 1.75
- cotangent: float32 [8192, 1536], P(('fsdp', 'ctx')), may hold values from -6 to 6
Outputs:
- block_out: float32 [8192, 1536], P(('fsdp', 'ctx'))
- grad_input: float32 [8192, 1536], P(('fsdp', 'ctx'))
- grad_in_weight: float32 [2, 1536, 6448], P(None, ('fsdp', 'ctx'))
- grad_out_weight: float32 [2, 3072, 1536], P(None, ('fsdp', 'ctx'))
- grad_norm_gain: float32 [2, 1536], replicated
- grad_conv_weight: float32 [2, 4, 3328], replicated
- grad_conv_bias: float32 [2, 3328], replicated
- grad_step_bias: float32 [2, 48], replicated
- grad_decay_log: float32 [2, 48], replicated
- grad_skip_gain: float32 [2, 48], replicated
- grad_gate_gain: float32 [2, 3072], replicated
The draws below stay inside these ranges and needn't reach their ends.
All inputs are finite; a program needn't handle non-finite values.
Results may differ from the reference program's by a relative error of at most 0.0097.
Values may be sent and summed in bfloat16 or wider, within the bound.
No kernel may reach another device: no remote copies, remote signals or barrier semaphores. Data moves between devices by JAX's collectives and lax.ppermute only.
A program may use at most 384 MiB of HBM per device.

```python
import jax
import jax.numpy as jnp
from jax import lax

D = 1536
H = 48
P_SIZE = 64
N = 128
CONV = 4
GROUP = 256
LAYERS = 2
DI = 3072
CC = 3328
E = 6448
LEN = 1024
SEQS = 8
TOKENS = 8192


def strengthened(array, key, source, target, shards_of, factor):
    owner, partner = [(jnp.arange(array.shape[axis_at]) // (array.shape[axis_at] // shards_of)).reshape([-1 if axis == axis_at else 1 for axis in range(array.ndim)]) for axis_at in (source, target)]
    chosen = jax.random.permutation(key, shards_of)[partner]
    strong = (owner == chosen) | (owner == (partner + shards_of // 2) % shards_of)
    return jnp.where(strong, factor * array, array)


def levels(key, extent, shards, low, high):
    level, own = 1.0, jax.random.fold_in(key, 6)
    for position, shards_of in shards:
        heights = jnp.exp(jax.random.uniform(jax.random.fold_in(own, position), (shards_of,), jnp.float32, low / len(shards), high / len(shards)))
        level = level * jnp.repeat(heights, extent[position] // shards_of).reshape([-1 if axis == position else 1 for axis in range(len(extent))])
    return level


def scatter_about(own_key, shape, width, limit, shards=(), held_as=jnp.bfloat16):
    factor_of = levels(own_key, shape, shards, -0.22, 0.18) if shards else 1.0
    values = jax.random.normal(own_key, shape, jnp.float32) * width * factor_of
    return jnp.minimum(jnp.maximum(values, -limit), limit).astype(held_as)


def gaussian_with(key, shape, width, most, cuts, heavy, held_as=jnp.bfloat16):
    values = width * jax.random.normal(key, shape, jnp.float32)
    if cuts:
        values = values * levels(key, shape, cuts, -0.22, 0.18)
    return jnp.clip(strengthened(values, jax.random.fold_in(key, 3), *heavy), -most, most).astype(held_as)


def setup_inputs(seed: int = 0) -> dict:
    splits = jax.random.split(jax.random.key(seed), 12)
    return {
        "activations": gaussian_with(splits[0], (TOKENS, D), 1.0, 6.0, ((0, 32),), (0, 1, 32, 2.75), jnp.float32),
        "in_weight": scatter_about(splits[1], (LAYERS, D, E), D ** -0.5, 0.15625, ((1, 8),)),
        "out_weight": scatter_about(splits[2], (LAYERS, DI, D), DI ** -0.5, 0.109375, ((1, 8),)),
        "norm_gain": jnp.clip(1.0 + 0.15 * jax.random.normal(splits[3], (LAYERS, D), jnp.float32), 0.25, 1.75),
        "conv_weight": scatter_about(splits[4], (LAYERS, CONV, CC), CONV ** -0.5, 3.0, (), jnp.float32),
        "conv_bias": scatter_about(splits[5], (LAYERS, CC), 0.5, 3.0, (), jnp.float32),
        "step_bias": jnp.clip(jax.random.uniform(splits[6], (LAYERS, H), jnp.float32, -9.0, -3.0), -9.0, -3.0),
        "decay_log": jnp.clip(jax.random.uniform(splits[7], (LAYERS, H), jnp.float32, -1.5, 2.0), -1.5, 2.0),
        "skip_gain": jnp.clip(jax.random.uniform(splits[8], (LAYERS, H), jnp.float32, 0.5, 1.5), 0.5, 1.5),
        "gate_gain": jnp.clip(1.0 + 0.15 * jax.random.normal(splits[9], (LAYERS, DI), jnp.float32), 0.25, 1.75),
        "cotangent": gaussian_with(splits[10], (TOKENS, D), 1.0, 6.0, ((0, 32),), (0, 1, 32, 2.75), jnp.float32),
    }


EPS = 1e-05
HIGH = lax.Precision.HIGHEST

def rms_norm(values, gain_row):
    return values * lax.rsqrt(lax.optimization_barrier(jnp.mean(values * values, axis=-1, keepdims=True)) + EPS) * gain_row

def gated_norm(ssm_out, gate_in, gain_row):
    gated = ssm_out * jax.nn.silu(gate_in)
    return gated * lax.rsqrt(lax.optimization_barrier(jnp.mean(gated * gated, axis=-1, keepdims=True)) + EPS) * gain_row

def conv_act(extended, taps, bias_row):
    length = extended.shape[0] - (CONV - 1)
    summed = jnp.zeros((length, extended.shape[1]), jnp.float32) + bias_row[None, :]
    for offset in range(CONV):
        summed = summed + extended[offset:offset + length] * taps[offset][None, :]
    return jax.nn.silu(summed)

def block_scan(x_heads, b_rows, c_rows, step_sizes, log_decay, skip_row, start):
    blocks = x_heads.shape[0] // GROUP
    x_blocks = x_heads.reshape(blocks, GROUP, H, P_SIZE)
    b_blocks = b_rows.reshape(blocks, GROUP, N)
    c_blocks = c_rows.reshape(blocks, GROUP, N)
    step_blocks = jnp.transpose(step_sizes.reshape(blocks, GROUP, H), (0, 2, 1))
    cum_decay = jnp.cumsum(jnp.transpose(log_decay.reshape(blocks, GROUP, H), (0, 2, 1)), axis=2)
    scores = jnp.einsum('bln,bsn->bls', c_blocks, b_blocks, precision=HIGH)
    causal = jnp.arange(GROUP)[:, None] >= jnp.arange(GROUP)[None, :]
    decay_gaps = cum_decay[:, :, :, None] - cum_decay[:, :, None, :]
    decays = jnp.where(causal, jnp.exp(jnp.where(causal, decay_gaps, 0.0)), 0.0)
    mixing = scores[:, None, :, :] * decays * step_blocks[:, :, None, :]
    intra_out = jnp.einsum('bhls,bshp->blhp', mixing, x_blocks, precision=HIGH)
    tail_weight = jnp.exp(cum_decay[:, :, -1:] - cum_decay) * step_blocks
    weighted = x_blocks * jnp.transpose(tail_weight, (0, 2, 1))[:, :, :, None]
    states = jnp.einsum('bshp,bsn->bhpn', weighted, b_blocks, precision=HIGH)
    totals = jnp.exp(cum_decay[:, :, -1])

    def advance(state_now, block_items):
        factor, new_state = block_items
        return (factor[:, None, None] * state_now + new_state, state_now)
    last_state, entering = lax.scan(advance, start, (totals, states))
    inter_out = jnp.einsum('bln,bhpn->blhp', c_blocks, entering, precision=HIGH)
    inter_out = inter_out * jnp.exp(jnp.transpose(cum_decay, (0, 2, 1)))[:, :, :, None]
    result = intra_out + inter_out + skip_row[None, None, :, None] * x_blocks
    return (result.reshape(blocks * GROUP, H * P_SIZE), last_state)

def mixer(activated, raw_steps, bias_row, log_row, skip_row, start):
    x_heads = activated[:, :DI].reshape(-1, H, P_SIZE)
    b_rows = activated[:, DI:DI + N]
    c_rows = activated[:, DI + N:]
    step_sizes = jax.nn.softplus(raw_steps + bias_row[None, :])
    log_decay = -step_sizes * jnp.exp(log_row)[None, :]
    return block_scan(x_heads, b_rows, c_rows, step_sizes, log_decay, skip_row, start)

def rows_product(left, right):
    return lax.dot_general(left, right, (((0,), (0,)), ((), ())), preferred_element_type=jnp.float32)

def right_transposed(left, right):
    return lax.dot_general(left, right, (((1,), (1,)), ((), ())), preferred_element_type=jnp.float32)

def one_sequence(seq_acts, seq_cotan, params):
    in_weight, out_weight, norm_gain, conv_weight, conv_bias, step_bias, decay_log, skip_gain, gate_gain = params
    stream = seq_acts
    saved = []
    for layer_index in range(LAYERS):
        normed = rms_norm(stream, norm_gain[layer_index]).astype(jnp.bfloat16)
        projected = jnp.dot(normed, in_weight[layer_index], preferred_element_type=jnp.float32)
        gate_in = projected[:, :DI]
        conv_in = projected[:, DI:DI + CC].astype(jnp.bfloat16)
        raw_steps = projected[:, DI + CC:]
        extended = jnp.concatenate([jnp.zeros((CONV - 1, CC), jnp.float32), conv_in.astype(jnp.float32)], 0)
        activated = conv_act(extended, conv_weight[layer_index], conv_bias[layer_index])
        ssm_out, unused_state = mixer(activated, raw_steps, step_bias[layer_index], decay_log[layer_index], skip_gain[layer_index], jnp.zeros((H, P_SIZE, N), jnp.float32))
        gnormed = gated_norm(ssm_out, gate_in, gate_gain[layer_index]).astype(jnp.bfloat16)
        saved.append((stream, normed, gate_in, extended, activated, raw_steps, ssm_out, gnormed))
        stream = stream + jnp.dot(gnormed, out_weight[layer_index], preferred_element_type=jnp.float32)
    seq_out = stream
    grad_stream = seq_cotan
    collected = []
    for layer_index in reversed(range(LAYERS)):
        stream_in, normed, gate_in, extended, activated, raw_steps, ssm_out, gnormed = saved[layer_index]
        grad_bf = grad_stream.astype(jnp.bfloat16)
        grad_wout = rows_product(gnormed, grad_bf)
        d_gnormed = right_transposed(grad_bf, out_weight[layer_index])
        unused_out, pullback = jax.vjp(gated_norm, ssm_out, gate_in, gate_gain[layer_index])
        d_ssm, d_gate, g_gate = pullback(d_gnormed)
        zero_state = jnp.zeros((H, P_SIZE, N), jnp.float32)

        def mix_only(act_in, steps_in, bias_in, log_in, skip_in):
            return mixer(act_in, steps_in, bias_in, log_in, skip_in, zero_state)
        unused_mix, pullback = jax.vjp(mix_only, activated, raw_steps, step_bias[layer_index], decay_log[layer_index], skip_gain[layer_index])
        d_act, d_steps, g_bias, g_log, g_skip = pullback((d_ssm, jnp.zeros((H, P_SIZE, N), jnp.float32)))
        unused_act, pullback = jax.vjp(conv_act, extended, conv_weight[layer_index], conv_bias[layer_index])
        d_ext, g_taps, g_cbias = pullback(d_act)
        d_conv_in = d_ext[CONV - 1:]
        d_proj = jnp.concatenate([d_gate, d_conv_in, d_steps], 1).astype(jnp.bfloat16)
        grad_win = rows_product(normed, d_proj)
        d_normed = right_transposed(d_proj, in_weight[layer_index])
        unused_norm, pullback = jax.vjp(rms_norm, stream_in, norm_gain[layer_index])
        d_stream, g_norm = pullback(d_normed)
        grad_stream = grad_stream + d_stream
        collected.append((grad_win, grad_wout, g_norm, g_taps, g_cbias, g_bias, g_log, g_skip, g_gate))
    collected = collected[::-1]
    stacked = tuple((jnp.stack([entry[member] for entry in collected], 0) for member in range(9)))
    return (seq_out, grad_stream, stacked)

def reference(activations, in_weight, out_weight, norm_gain, conv_weight, conv_bias, step_bias, decay_log, skip_gain, gate_gain, cotangent):
    params = (in_weight, out_weight, norm_gain, conv_weight, conv_bias, step_bias, decay_log, skip_gain, gate_gain)
    acts_seqs = activations.reshape(SEQS, LEN, D)
    cotan_seqs = cotangent.reshape(SEQS, LEN, D)
    initial = tuple((jnp.zeros(param_array.shape, jnp.float32) for param_array in params))

    def visit(sums, seq_pair):
        seq_out, seq_grad, stacked = one_sequence(seq_pair[0], seq_pair[1], params)
        return (jax.tree.map(jnp.add, sums, stacked), (seq_out, seq_grad))
    totals, (outs_all, grads_all) = lax.scan(visit, initial, (acts_seqs, cotan_seqs))
    return (outs_all.reshape(TOKENS, D), grads_all.reshape(TOKENS, D), totals[0], totals[1], totals[2], totals[3], totals[4], totals[5], totals[6], totals[7], totals[8])
```

```python
import functools

import jax
import jax.numpy as jnp
from jax import lax
from jax.experimental import pallas as pl
from jax.experimental.pallas import tpu as pltpu
from jax.sharding import PartitionSpec as P

H = 48
P_SIZE = 64
N = 128
CONV = 4
LAYERS = 2
DI = 3072
CC = 3328
W = 256
G = DI // W
K = W // P_SIZE

EPS = 1e-05
HIGH = lax.Precision.HIGHEST
F32 = jnp.float32
BF = jnp.bfloat16


def mm(a, b):
    return lax.dot_general(a.astype(BF), b.astype(BF), (((1,), (0,)), ((), ())), preferred_element_type=F32)


def mm_nt(a, b):
    return lax.dot_general(a.astype(BF), b.astype(BF), (((1,), (1,)), ((), ())), preferred_element_type=F32)


def mm_tn(a, b):
    return lax.dot_general(a.astype(BF), b.astype(BF), (((0,), (0,)), ((), ())), preferred_element_type=F32)


def extend(halo_ref, conv_ref):
    return jnp.concatenate([halo_ref[...], conv_ref[...].astype(F32)], 0)


def conv_pre(ext, taps_ref, bias_ref, rows):
    acc = bias_ref[...] + ext[5 : 5 + rows] * taps_ref[0:1, :]
    for j in range(1, CONV):
        acc = acc + ext[5 + j : 5 + j + rows] * taps_ref[j : j + 1, :]
    return acc


def sigmoid(v):
    return 1.0 / (1.0 + jnp.exp(-v))


def pair_cols(col, first, low):
    return jnp.where(low, col[:, first : first + 1], col[:, first + 1 : first + 2])


def masked_scores(c_rows, b_rows):
    s = mm_nt(c_rows, b_rows)
    r = lax.broadcasted_iota(jnp.int32, s.shape, 0)
    q = lax.broadcasted_iota(jnp.int32, s.shape, 1)
    return jnp.where(r >= q, s, 0.0)


def scan_fwd_kernel(conv_ref, conv_bc_ref, halo_ref, halo_bc_ref, taps_ref, taps_bc_ref, bias_ref, bias_bc_ref,
                    col_ref, row_ref, skip_ref, y_ref, state_ref, bc_ref, s_ref):
    rows = conv_ref.shape[0]

    @pl.when(pl.program_id(0) == 0)
    def _():
        pre = conv_pre(extend(halo_bc_ref, conv_bc_ref), taps_bc_ref, bias_bc_ref, rows)
        bc = pre * sigmoid(pre)
        bc_ref[...] = bc
        s_ref[...] = masked_scores(bc[:, N:], bc[:, :N])

    pre = conv_pre(extend(halo_ref, conv_ref), taps_ref, bias_ref, rows)
    x = pre * sigmoid(pre)
    low = lax.broadcasted_iota(jnp.int32, (rows, 2 * P_SIZE), 1) < P_SIZE
    col = col_ref[0]
    row = row_ref[0]
    b_bf = bc_ref[:, :N].astype(BF)
    for pair in range(K // 2):
        h0 = 2 * pair
        cols = slice(pair * 128, pair * 128 + 128)
        x2 = x[:, cols]
        xs = x2 * pair_cols(col, K + h0, low)
        mixes, parts = [], []
        for i in range(2):
            h = h0 + i
            decay = jnp.exp(jnp.minimum(col[:, h : h + 1] - row[h : h + 1, :], 0.0))
            mixes.append((s_ref[...] * decay).astype(BF))
            parts.append(jnp.where(low if i == 0 else ~low, xs, 0.0).astype(BF))
        y = mm(jnp.concatenate(mixes, 1), jnp.concatenate(parts, 0))
        y_ref[:, cols] = y + skip_ref[:, cols] * x2
        last = jnp.where(low[:1], row[h0 : h0 + 1, rows - 1 : rows], row[h0 + 1 : h0 + 2, rows - 1 : rows])
        tail = jnp.exp(last - pair_cols(col, h0, low))
        state_ref[cols, :] = mm_tn(xs * tail, b_bf)


def gate_fwd_kernel(y_ref, gate_ref, in_ref, bc_ref, col_ref, gain_ref, ssm_ref, gn_ref, gated_ref, acc_ref):
    g = pl.program_id(0)
    rows = y_ref.shape[0]

    @pl.when(g == 0)
    def _():
        acc_ref[...] = jnp.zeros_like(acc_ref)

    low = lax.broadcasted_iota(jnp.int32, (rows, 2 * P_SIZE), 1) < P_SIZE
    col = col_ref[0]
    z = mm_nt(bc_ref[:, N:], in_ref[...])
    e = jnp.concatenate([jnp.exp(pair_cols(col, 2 * p, low)) for p in range(K // 2)], 1)
    ssm = y_ref[...] + e * z
    ssm_ref[...] = ssm
    gate = gate_ref[...]
    gated = ssm * (gate * sigmoid(gate))
    gated_ref[g] = gated
    acc_ref[...] += gated * gated

    @pl.when(g == G - 1)
    def _():
        r = lax.rsqrt(jnp.sum(acc_ref[...], 1, keepdims=True) / DI + EPS)
        for i in range(G):
            cols = slice(i * W, i * W + W)
            gn_ref[:, cols] = (gated_ref[i] * r * gain_ref[:, cols]).astype(BF)


def gate_bwd_kernel(ssm_ref, gate_ref, dn_ref, gain_ref, col_ref, bc_ref, dssm_ref, dgate_ref, ggain_ref, lg_ref,
                    sq_ref, dot_ref, r_ref, k_ref):
    phase = pl.program_id(0)
    g = pl.program_id(1)
    rows = ssm_ref.shape[0]
    ssm = ssm_ref[...]
    gate = gate_ref[...]
    sig = sigmoid(gate)
    act = gate * sig
    gated = ssm * act
    dn = dn_ref[...]
    dng = dn * gain_ref[...]

    @pl.when((phase == 0) & (g == 0))
    def _():
        sq_ref[...] = jnp.zeros_like(sq_ref)
        dot_ref[...] = jnp.zeros_like(dot_ref)

    @pl.when(phase == 0)
    def _():
        sq_ref[...] += gated * gated
        dot_ref[...] += dng * gated

    @pl.when((phase == 1) & (g == 0))
    def _():
        r = lax.rsqrt(jnp.sum(sq_ref[...], 1, keepdims=True) / DI + EPS)
        r_ref[...] = r
        k_ref[...] = r * r * r * jnp.sum(dot_ref[...], 1, keepdims=True) / DI

    @pl.when(phase == 1)
    def _():
        r = r_ref[...]
        dgated = r * dng - gated * k_ref[...]
        dssm = dgated * act
        dssm_ref[...] = dssm
        dgate_ref[...] = (dgated * ssm * (sig * (1.0 + gate * (1.0 - sig)))).astype(BF)
        ggain_ref[...] = jnp.sum(dn * (gated * r), 0, keepdims=True)
        low = lax.broadcasted_iota(jnp.int32, (rows, 2 * P_SIZE), 1) < P_SIZE
        col = col_ref[0]
        e = jnp.concatenate([jnp.exp(pair_cols(col, 2 * p, low)) for p in range(K // 2)], 1)
        lg_ref[...] = mm_tn(dssm * e, bc_ref[:, N:])


def conv_back(d_act, pre, sig, ext, taps_ref, rows):
    d_pre = d_act * (sig * (1.0 + pre * (1.0 - sig)))
    zero = jnp.zeros((8, d_pre.shape[1]), F32)
    below = jnp.concatenate([d_pre, zero], 0)
    above = jnp.concatenate([zero, d_pre[:8]], 0)
    d_conv = below[3 : 3 + rows] * taps_ref[0:1, :]
    edge = above[8:16] * taps_ref[0:1, :]
    terms = [jnp.sum(d_pre * ext[5 : 5 + rows], 0, keepdims=True)]
    for j in range(1, CONV):
        d_conv = d_conv + below[3 - j : 3 - j + rows] * taps_ref[j : j + 1, :]
        edge = edge + above[8 - j : 16 - j] * taps_ref[j : j + 1, :]
        terms.append(jnp.sum(d_pre * ext[5 + j : 5 + j + rows], 0, keepdims=True))
    terms.append(jnp.sum(d_pre, 0, keepdims=True))
    return d_conv, edge, terms


def scan_bwd_kernel(conv_ref, conv_bc_ref, halo_ref, halo_bc_ref, taps_ref, taps_bc_ref, bias_ref, bias_bc_ref,
                    col_ref, row_ref, skip_ref, bc_ref, dy_ref, in_ref, out_ref,
                    dconv_ref, edge_ref, gt_ref, dconv_bc_ref, edge_bc_ref, gt_bc_ref, colo_ref, rowo_ref, misc_ref,
                    s_ref, ds_ref, dbc_ref):
    g = pl.program_id(0)
    rows = conv_ref.shape[0]

    @pl.when(g == 0)
    def _():
        s_ref[...] = masked_scores(bc_ref[:, N:], bc_ref[:, :N])
        ds_ref[...] = jnp.zeros_like(ds_ref)
        dbc_ref[...] = jnp.zeros_like(dbc_ref)

    ext = extend(halo_ref, conv_ref)
    pre = conv_pre(ext, taps_ref, bias_ref, rows)
    sig = sigmoid(pre)
    x = pre * sig
    low = lax.broadcasted_iota(jnp.int32, (rows, 2 * P_SIZE), 1) < P_SIZE
    lane = lax.broadcasted_iota(jnp.int32, (rows, 2 * K), 1)
    col = col_ref[0]
    row = row_ref[0]
    b_bf = bc_ref[:, :N].astype(BF)
    c_bf = bc_ref[:, N:].astype(BF)
    colo = jnp.zeros((rows, 2 * K), F32)
    dxs = []
    misc_ref[...] = jnp.zeros_like(misc_ref)
    rowo_ref[...] = jnp.zeros_like(rowo_ref)
    for pair in range(K // 2):
        h0 = 2 * pair
        cols = slice(pair * 128, pair * 128 + 128)
        x2 = x[:, cols]
        step = pair_cols(col, K + h0, low)
        xs = x2 * step
        xs_bf = xs.astype(BF)
        dy = dy_ref[:, cols]
        h_in = in_ref[cols, :]
        h_out = out_ref[cols, :]
        cum = pair_cols(col, h0, low)
        e = jnp.exp(cum)
        last = jnp.where(low[:1], row[h0 : h0 + 1, rows - 1 : rows], row[h0 + 1 : h0 + 2, rows - 1 : rows])
        tail = jnp.exp(last - cum)
        edy = e * dy
        txs = tail * xs
        inter = edy * mm_nt(c_bf, h_in)
        u = mm_nt(b_bf, h_out)
        r = txs * u
        dbc_ref[:, N:] += mm(edy, h_in)
        dbc_ref[:, :N] += mm(txs, h_out)
        d_xs = tail * u
        side = inter - r
        for i in range(2):
            h = h0 + i
            keep = low if i == 0 else ~low
            dyh = jnp.where(keep, dy, 0.0).astype(BF)
            d_mix = mm_nt(dyh, xs_bf)
            decay = jnp.exp(jnp.minimum(col[:, h : h + 1] - row[h : h + 1, :], 0.0))
            d_ld = d_mix * decay
            ds_ref[...] += d_ld
            s = s_ref[...]
            weight = d_ld * s
            d_xs = d_xs + mm_tn(s * decay, dyh)
            rowo_ref[0, h : h + 1, :] = jnp.sum(weight, 0, keepdims=True)
            folded = weight[:, :128] + weight[:, 128:] + jnp.where(keep, side, 0.0)
            colo = jnp.where(lane == h, jnp.sum(folded, 1, keepdims=True), colo)
        prod = x2 * d_xs
        for i in range(2):
            keep = low if i == 0 else ~low
            s_sum = jnp.sum(jnp.where(keep, prod, 0.0), 1, keepdims=True)
            colo = jnp.where(lane == K + h0 + i, s_sum, colo)
        dxs.append(step * d_xs + skip_ref[:, cols] * dy)
        hg = h_in.astype(F32) * h_out.astype(F32)
        misc_ref[0, 0:1, cols] = jnp.sum(dy * x2, 0, keepdims=True)
        misc_ref[0, 1:2, cols] = jnp.sum(r, 0, keepdims=True)
        misc_ref[0, 2:3, cols] = jnp.sum(hg[:P_SIZE], 0, keepdims=True)
        misc_ref[0, 3:4, cols] = jnp.sum(hg[P_SIZE:], 0, keepdims=True)
    colo_ref[0] = colo
    d_conv, edge, terms = conv_back(jnp.concatenate(dxs, 1), pre, sig, ext, taps_ref, rows)
    dconv_ref[...] = d_conv
    edge_ref[...] = edge
    gt_ref[...] = jnp.zeros_like(gt_ref)
    for j, term in enumerate(terms):
        gt_ref[j : j + 1, :] = term

    @pl.when(g == G - 1)
    def _():
        r_i = lax.broadcasted_iota(jnp.int32, ds_ref.shape, 0)
        q_i = lax.broadcasted_iota(jnp.int32, ds_ref.shape, 1)
        ds = jnp.where(r_i >= q_i, ds_ref[...], 0.0).astype(BF)
        d_c = dbc_ref[:, N:] + mm(ds, b_bf)
        d_b = dbc_ref[:, :N] + mm_tn(ds, c_bf)
        ext2 = extend(halo_bc_ref, conv_bc_ref)
        pre2 = conv_pre(ext2, taps_bc_ref, bias_bc_ref, rows)
        d_conv2, edge2, terms2 = conv_back(
            jnp.concatenate([d_b, d_c], 1), pre2, sigmoid(pre2), ext2, taps_bc_ref, rows)
        dconv_bc_ref[...] = d_conv2
        edge_bc_ref[...] = edge2
        gt_bc_ref[...] = jnp.zeros_like(gt_bc_ref)
        for j, term in enumerate(terms2):
            gt_bc_ref[j : j + 1, :] = term


def col_block(rows):
    return pl.BlockSpec((rows, W), lambda g: (0, g))


def bc_block(rows):
    return pl.BlockSpec((rows, W), lambda g: (0, G))


def fixed(shape):
    return pl.BlockSpec(shape, lambda g: (0,) * len(shape))


def packs(rows):
    return [pl.BlockSpec((1, rows, 2 * K), lambda g: (g, 0, 0)), pl.BlockSpec((1, 2 * K, rows), lambda g: (g, 0, 0))]


def conv_specs(rows):
    return [col_block(rows), bc_block(rows), col_block(8), bc_block(8), col_block(CONV), bc_block(CONV),
            col_block(1), bc_block(1)] + packs(rows) + [col_block(1)]


STATE = pl.BlockSpec((W, N), lambda g: (g, 0))


def sds(shape, dtype=F32):
    return jax.ShapeDtypeStruct(shape, dtype)


def scan_fwd(conv_in, halo, taps, bias, col, row, skip):
    rows = conv_in.shape[0]
    return pl.pallas_call(
        scan_fwd_kernel,
        grid=(G,),
        in_specs=conv_specs(rows),
        out_specs=[col_block(rows), STATE, fixed((rows, 2 * N))],
        out_shape=[sds((rows, DI)), sds((DI, N)), sds((rows, 2 * N))],
        scratch_shapes=[pltpu.VMEM((rows, rows), F32)],
        name="scan_fwd",
    )(conv_in, conv_in, halo, halo, taps, taps, bias, bias, col, row, skip)


def gate_fwd(y, gate, incoming, bc, col, gain):
    rows = y.shape[0]
    return pl.pallas_call(
        gate_fwd_kernel,
        grid=(G,),
        in_specs=[col_block(rows), col_block(rows), STATE, fixed((rows, 2 * N)), packs(rows)[0], fixed((1, DI))],
        out_specs=[col_block(rows), fixed((rows, DI))],
        out_shape=[sds((rows, DI)), sds((rows, DI), BF)],
        scratch_shapes=[pltpu.VMEM((G, rows, W), F32), pltpu.VMEM((rows, W), F32)],
        name="gate_fwd",
    )(y, gate, incoming, bc, col, gain)


def gate_bwd(ssm, gate, dn, gain, col, bc):
    rows = ssm.shape[0]
    block = pl.BlockSpec((rows, W), lambda p, g: (0, g))
    late = pl.BlockSpec((rows, W), lambda p, g: (0, p * g))
    return pl.pallas_call(
        gate_bwd_kernel,
        grid=(2, G),
        in_specs=[block, block, block, pl.BlockSpec((1, W), lambda p, g: (0, g)),
                  pl.BlockSpec((1, rows, 2 * K), lambda p, g: (g, 0, 0)),
                  pl.BlockSpec((rows, 2 * N), lambda p, g: (0, 0))],
        out_specs=[late, late, pl.BlockSpec((1, W), lambda p, g: (0, p * g)),
                   pl.BlockSpec((W, N), lambda p, g: (p * g, 0))],
        out_shape=[sds((rows, DI)), sds((rows, DI), BF), sds((1, DI)), sds((DI, N))],
        scratch_shapes=[pltpu.VMEM((rows, W), F32), pltpu.VMEM((rows, W), F32),
                        pltpu.VMEM((rows, 1), F32), pltpu.VMEM((rows, 1), F32)],
        name="gate_bwd",
    )(ssm, gate, dn, gain, col, bc)


def scan_bwd(conv_in, halo, taps, bias, col, row, skip, bc, dy, incoming, outgoing):
    rows = conv_in.shape[0]
    return pl.pallas_call(
        scan_bwd_kernel,
        grid=(G,),
        in_specs=conv_specs(rows) + [fixed((rows, 2 * N)), col_block(rows), STATE, STATE],
        out_specs=[col_block(rows), col_block(8), col_block(8), fixed((rows, W)), fixed((8, W)), fixed((8, W))]
        + packs(rows) + [pl.BlockSpec((1, 8, W), lambda g: (g, 0, 0))],
        out_shape=[sds((rows, DI)), sds((8, DI)), sds((8, DI)), sds((rows, W)), sds((8, W)), sds((8, W)),
                   sds((G, rows, 2 * K)), sds((G, 2 * K, rows)), sds((G, 8, W))],
        scratch_shapes=[pltpu.VMEM((rows, rows), F32), pltpu.VMEM((rows, rows), F32), pltpu.VMEM((rows, 2 * N), F32)],
        name="scan_bwd",
    )(conv_in, conv_in, halo, halo, taps, taps, bias, bias, col, row, skip, bc, dy, incoming, outgoing)


def passed_along(value, axis, steps):
    count = lax.axis_size(axis)
    initial, last = (max(0, -steps), min(count, count - steps))
    return lax.ppermute(value, axis, [(source, source + steps) for source in range(initial, last)])


CHUNKS = 2


def carry(totals, local_state, steps):
    hops = lax.axis_size("ctx") - 1
    size = DI // CHUNKS
    parts = []
    for chunk in range(CHUNKS):
        rows = slice(chunk * size, chunk * size + size)
        own, factor = local_state[rows], totals[rows]
        incoming = passed_along(own.astype(BF), "ctx", steps)
        for _ in range(hops - 1):
            incoming = passed_along((factor * incoming.astype(F32) + own).astype(BF), "ctx", steps)
        parts.append(incoming)
    return jnp.concatenate(parts, 0)


def all_sum(value):
    for axis in ("fsdp", "ctx"):
        count = lax.axis_size(axis)
        if count & (count - 1):
            value = lax.psum(value, axis)
            continue
        bit = 1
        while bit < count:
            value = value + lax.ppermute(value, axis, [(i, i ^ bit) for i in range(count)])
            bit *= 2
    return value


def rms_norm(values, gain_row):
    return values * lax.rsqrt(jnp.mean(values * values, axis=-1, keepdims=True) + EPS) * gain_row


def rows_product(left, right):
    return lax.dot_general(left, right, (((0,), (0,)), ((), ())), preferred_element_type=F32)


def right_transposed(left, right):
    return lax.dot_general(left, right, (((1,), (1,)), ((), ())), preferred_element_type=F32)


def weight_gradients(normed, d_proj, gnormed, grad_bf):
    tok_rows = normed.shape[0]
    fsdp_count = lax.axis_size("fsdp")
    ctx_count = lax.axis_size("ctx")
    width_in = d_proj.shape[1]
    inner = gnormed.shape[1]
    tile_rows = inner // (fsdp_count * ctx_count)
    all_rows = (
        lax.all_gather(normed, "ctx", axis=0, tiled=True),
        lax.all_gather(grad_bf, "ctx", axis=0, tiled=True),
    )
    proj_split = d_proj.reshape(tok_rows, 1, ctx_count, width_in // ctx_count)
    gate_split = gnormed.reshape(tok_rows, fsdp_count, ctx_count, tile_rows)
    cols = (
        lax.all_to_all(proj_split, "ctx", split_axis=2, concat_axis=0, tiled=True),
        lax.all_to_all(gate_split, "ctx", split_axis=2, concat_axis=0, tiled=True),
    )
    proj_cols = cols[0].reshape(ctx_count * tok_rows, width_in // ctx_count)
    gate_cols = cols[1].reshape(ctx_count * tok_rows, fsdp_count * tile_rows)
    part_in = rows_product(all_rows[0], proj_cols)
    part_out = rows_product(gate_cols, all_rows[1])
    summed = (
        lax.psum_scatter(part_in, "fsdp", scatter_dimension=0, tiled=True),
        lax.psum_scatter(part_out, "fsdp", scatter_dimension=0, tiled=True),
    )
    owned_in = lax.all_to_all(summed[0], "ctx", split_axis=0, concat_axis=1, tiled=True)
    return (owned_in, summed[1])


def grouped(cum, steps):
    rows = cum.shape[0]
    both = jnp.stack([cum.reshape(rows, G, K), steps.reshape(rows, G, K)], 2).reshape(rows, G, 2 * K)
    return jnp.transpose(both, (1, 0, 2)), jnp.transpose(both, (1, 2, 0))


def local(
    activations,
    in_weight,
    out_weight,
    norm_gain,
    conv_weight,
    conv_bias,
    step_bias,
    decay_log,
    skip_gain,
    gate_gain,
    cotangent,
):
    rows = activations.shape[0]
    edge_count = CONV - 1
    order = jnp.arange(rows)
    lower = (order[:, None] >= order[None, :]).astype(F32)
    weights = []
    for k in range(LAYERS):
        weights.append(
            (
                lax.all_gather(in_weight[k][:, DI:], "fsdp", axis=0, tiled=True),
                lax.all_gather(in_weight[k][:, :DI], "fsdp", axis=0, tiled=True),
                lax.all_gather(out_weight[k], "fsdp", axis=0, tiled=True),
            )
        )
    stream = activations
    kept = []
    for k in range(LAYERS):
        w_conv, w_gate, w_out = weights[k]
        normed = rms_norm(stream, norm_gain[k]).astype(BF)
        proj = jnp.dot(normed, w_conv, preferred_element_type=F32)
        conv_in = proj[:, :CC].astype(BF)
        raw_steps = proj[:, CC:]
        edge_in = passed_along(conv_in[rows - edge_count :], "ctx", 1)
        halo = jnp.concatenate([jnp.zeros((8 - edge_count, CC), F32), edge_in.astype(F32)], 0)
        steps = jax.nn.softplus(raw_steps + step_bias[k][None, :])
        cum = jnp.dot(lower, -steps * jnp.exp(decay_log[k])[None, :], precision=HIGH)
        col, row = grouped(cum, steps)
        totals = jnp.repeat(jnp.exp(cum[-1]), P_SIZE)[:, None]
        skip = jnp.repeat(skip_gain[k], P_SIZE)[None, :]
        bias = conv_bias[k][None, :]
        y, state, bc = scan_fwd(conv_in, halo, conv_weight[k], bias, col, row, skip)
        gate_in = jnp.dot(normed, w_gate, preferred_element_type=F32)
        incoming = carry(totals, state, 1)
        ssm, gnormed = gate_fwd(y, gate_in, incoming, bc, col, gate_gain[k][None, :])
        kept.append((stream, normed, gate_in, conv_in, halo, raw_steps, steps, col, row, totals, skip, bias, bc,
                     incoming, ssm, gnormed))
        stream = stream + jnp.dot(gnormed, w_out, preferred_element_type=F32)
    grad_stream = cotangent
    collected = []
    for k in reversed(range(LAYERS)):
        w_conv, w_gate, w_out = weights[k]
        (stream_in, normed, gate_in, conv_in, halo, raw_steps, steps, col, row, totals, skip, bias, bc,
         incoming, ssm, gnormed) = kept[k]
        grad_bf = grad_stream.astype(BF)
        d_gnormed = right_transposed(grad_bf, w_out)
        d_ssm, d_gate, g_gate, local_grad = gate_bwd(ssm, gate_in, d_gnormed, gate_gain[k][None, :], col, bc)
        outgoing = carry(totals, local_grad, -1)
        d_x, edge_x, gt_x, d_bc, edge_bc, gt_bc, colo, rowo, misc = scan_bwd(
            conv_in, halo, conv_weight[k], bias, col, row, skip, bc, d_ssm, incoming, outgoing)
        edges = jnp.concatenate([edge_x[:edge_count], edge_bc[:edge_count]], 1)
        edge_back = passed_along(edges, "ctx", -1)
        taps_grad = jnp.concatenate([gt_x, gt_bc], 1)
        colf = jnp.transpose(colo, (1, 0, 2))
        d_cum = colf[:, :, :K].reshape(rows, H) - jnp.transpose(rowo[:, :K], (2, 0, 1)).reshape(rows, H)
        g_skip = misc[:, 0].reshape(H, P_SIZE).sum(1)
        r_sum = misc[:, 1].reshape(H, P_SIZE).sum(1)
        hg = jnp.transpose(misc[:, 2:4].reshape(G, 2, 2, N), (0, 2, 1, 3)).sum(-1).reshape(H)
        d_last = r_sum + totals[::P_SIZE, 0] * hg
        d_cum = d_cum + jnp.where(order[:, None] == rows - 1, d_last[None, :], 0.0)
        d_log = jnp.dot(lower.T, d_cum, precision=HIGH)
        rate = jnp.exp(decay_log[k])[None, :]
        d_step = colf[:, :, K:].reshape(rows, H) - d_log * rate
        d_raw = d_step * jax.nn.sigmoid(raw_steps + step_bias[k][None, :])
        g_bias = d_raw.sum(0)
        g_log = -(d_log * steps * rate).sum(0)
        d_conv = jnp.concatenate([d_x, d_bc], 1)
        d_conv = d_conv + jnp.pad(edge_back, ((rows - edge_count, 0), (0, 0)))
        d_rest = jnp.concatenate([d_conv, d_raw], 1).astype(BF)
        d_normed = right_transposed(d_gate, w_gate) + right_transposed(d_rest, w_conv)
        _, pullback = jax.vjp(rms_norm, stream_in, norm_gain[k])
        d_stream, g_norm = pullback(d_normed)
        grad_stream = grad_stream + d_stream
        owned_in, owned_out = weight_gradients(normed, jnp.concatenate([d_gate, d_rest], 1), gnormed, grad_bf)
        small = [g_norm, taps_grad[:CONV].reshape(-1), taps_grad[CONV], g_bias, g_log, g_skip, g_gate.reshape(-1)]
        sizes = [part.shape[0] for part in small]
        flat = jnp.concatenate(small)
        flat = all_sum(jnp.pad(flat, (0, -flat.shape[0] % 1024)).reshape(-1, 128)).reshape(-1)
        parts, at = [], 0
        for size in sizes:
            parts.append(flat[at : at + size])
            at += size
        parts[1] = parts[1].reshape(CONV, CC)
        collected.append((owned_in, owned_out, *parts))
    collected = collected[::-1]
    stacked = [jnp.stack([entry[member] for entry in collected], 0) for member in range(9)]
    return (stream, grad_stream, *stacked)


def solution(mesh):
    tokens = P(("fsdp", "ctx"), None)
    sharded = P(None, "fsdp", None)
    owned = P(None, ("fsdp", "ctx"), None)
    return jax.shard_map(
        local,
        mesh=mesh,
        in_specs=(tokens, sharded, sharded) + (P(),) * 7 + (tokens,),
        out_specs=(tokens, tokens, owned, owned) + (P(),) * 7,
        check_vma=False,
    )
```

```python
import functools

import jax
import jax.numpy as jnp
from jax import lax
from jax.experimental import pallas as pl
from jax.experimental.pallas import tpu as pltpu
from jax.sharding import PartitionSpec as P

H = 48
P_SIZE = 64
N = 128
CONV = 4
LAYERS = 2
DI = 3072
CC = 3328
W = 256
G = DI // W
K = W // P_SIZE

EPS = 1e-05
HIGH = lax.Precision.HIGHEST
F32 = jnp.float32
BF = jnp.bfloat16


def mm(a, b):
    return lax.dot_general(a.astype(BF), b.astype(BF), (((1,), (0,)), ((), ())), preferred_element_type=F32)


def mm_nt(a, b):
    return lax.dot_general(a.astype(BF), b.astype(BF), (((1,), (1,)), ((), ())), preferred_element_type=F32)


def mm_tn(a, b):
    return lax.dot_general(a.astype(BF), b.astype(BF), (((0,), (0,)), ((), ())), preferred_element_type=F32)


def extend(halo_ref, conv_ref):
    return jnp.concatenate([halo_ref[...], conv_ref[...].astype(F32)], 0)


def conv_pre(ext, taps_ref, bias_ref, rows):
    acc = bias_ref[...] + ext[5 : 5 + rows] * taps_ref[0:1, :]
    for j in range(1, CONV):
        acc = acc + ext[5 + j : 5 + j + rows] * taps_ref[j : j + 1, :]
    return acc


def sigmoid(v):
    return 1.0 / (1.0 + jnp.exp(-v))


def pair_cols(col, first, low):
    return jnp.where(low, col[:, first : first + 1], col[:, first + 1 : first + 2])


def masked_scores(c_rows, b_rows):
    s = mm_nt(c_rows, b_rows)
    r = lax.broadcasted_iota(jnp.int32, s.shape, 0)
    q = lax.broadcasted_iota(jnp.int32, s.shape, 1)
    return jnp.where(r >= q, s, 0.0)


def scan_fwd_kernel(conv_ref, conv_bc_ref, halo_ref, halo_bc_ref, taps_ref, taps_bc_ref, bias_ref, bias_bc_ref,
                    col_ref, row_ref, skip_ref, y_ref, state_ref, bc_ref, s_ref):
    rows = conv_ref.shape[0]

    @pl.when(pl.program_id(0) == 0)
    def _():
        pre = conv_pre(extend(halo_bc_ref, conv_bc_ref), taps_bc_ref, bias_bc_ref, rows)
        bc = pre * sigmoid(pre)
        bc_ref[...] = bc
        s_ref[...] = masked_scores(bc[:, N:], bc[:, :N])

    pre = conv_pre(extend(halo_ref, conv_ref), taps_ref, bias_ref, rows)
    x = pre * sigmoid(pre)
    low = lax.broadcasted_iota(jnp.int32, (rows, 2 * P_SIZE), 1) < P_SIZE
    col = col_ref[0]
    row = row_ref[0]
    b_bf = bc_ref[:, :N].astype(BF)
    for pair in range(K // 2):
        h0 = 2 * pair
        cols = slice(pair * 128, pair * 128 + 128)
        x2 = x[:, cols]
        xs = x2 * pair_cols(col, K + h0, low)
        mixes, parts = [], []
        for i in range(2):
            h = h0 + i
            decay = jnp.exp(jnp.minimum(col[:, h : h + 1] - row[h : h + 1, :], 0.0))
            mixes.append((s_ref[...] * decay).astype(BF))
            parts.append(jnp.where(low if i == 0 else ~low, xs, 0.0).astype(BF))
        y = mm(jnp.concatenate(mixes, 1), jnp.concatenate(parts, 0))
        y_ref[:, cols] = y + skip_ref[:, cols] * x2
        last = jnp.where(low[:1], row[h0 : h0 + 1, rows - 1 : rows], row[h0 + 1 : h0 + 2, rows - 1 : rows])
        tail = jnp.exp(last - pair_cols(col, h0, low))
        state_ref[cols, :] = mm_tn(xs * tail, b_bf)


def gate_fwd_kernel(y_ref, gate_ref, in_ref, bc_ref, col_ref, gain_ref, ssm_ref, gn_ref, gated_ref, acc_ref):
    g = pl.program_id(0)
    rows = y_ref.shape[0]

    @pl.when(g == 0)
    def _():
        acc_ref[...] = jnp.zeros_like(acc_ref)

    low = lax.broadcasted_iota(jnp.int32, (rows, 2 * P_SIZE), 1) < P_SIZE
    col = col_ref[0]
    z = mm_nt(bc_ref[:, N:], in_ref[...])
    e = jnp.concatenate([jnp.exp(pair_cols(col, 2 * p, low)) for p in range(K // 2)], 1)
    ssm = y_ref[...] + e * z
    ssm_ref[...] = ssm
    gate = gate_ref[...]
    gated = ssm * (gate * sigmoid(gate))
    gated_ref[g] = gated
    acc_ref[...] += gated * gated

    @pl.when(g == G - 1)
    def _():
        r = lax.rsqrt(jnp.sum(acc_ref[...], 1, keepdims=True) / DI + EPS)
        for i in range(G):
            cols = slice(i * W, i * W + W)
            gn_ref[:, cols] = (gated_ref[i] * r * gain_ref[:, cols]).astype(BF)


def gate_bwd_kernel(ssm_ref, gate_ref, dn_ref, gain_ref, col_ref, bc_ref, dssm_ref, dgate_ref, ggain_ref, lg_ref,
                    sq_ref, dot_ref, r_ref, k_ref):
    phase = pl.program_id(0)
    g = pl.program_id(1)
    rows = ssm_ref.shape[0]
    ssm = ssm_ref[...]
    gate = gate_ref[...]
    sig = sigmoid(gate)
    act = gate * sig
    gated = ssm * act
    dn = dn_ref[...]
    dng = dn * gain_ref[...]

    @pl.when((phase == 0) & (g == 0))
    def _():
        sq_ref[...] = jnp.zeros_like(sq_ref)
        dot_ref[...] = jnp.zeros_like(dot_ref)

    @pl.when(phase == 0)
    def _():
        sq_ref[...] += gated * gated
        dot_ref[...] += dng * gated

    @pl.when((phase == 1) & (g == 0))
    def _():
        r = lax.rsqrt(jnp.sum(sq_ref[...], 1, keepdims=True) / DI + EPS)
        r_ref[...] = r
        k_ref[...] = r * r * r * jnp.sum(dot_ref[...], 1, keepdims=True) / DI

    @pl.when(phase == 1)
    def _():
        r = r_ref[...]
        dgated = r * dng - gated * k_ref[...]
        dssm = dgated * act
        dssm_ref[...] = dssm
        dgate_ref[...] = (dgated * ssm * (sig * (1.0 + gate * (1.0 - sig)))).astype(BF)
        ggain_ref[...] = jnp.sum(dn * (gated * r), 0, keepdims=True)
        low = lax.broadcasted_iota(jnp.int32, (rows, 2 * P_SIZE), 1) < P_SIZE
        col = col_ref[0]
        e = jnp.concatenate([jnp.exp(pair_cols(col, 2 * p, low)) for p in range(K // 2)], 1)
        lg_ref[...] = mm_tn(dssm * e, bc_ref[:, N:])


def conv_back(d_act, pre, sig, ext, taps_ref, rows):
    d_pre = d_act * (sig * (1.0 + pre * (1.0 - sig)))
    zero = jnp.zeros((8, d_pre.shape[1]), F32)
    below = jnp.concatenate([d_pre, zero], 0)
    above = jnp.concatenate([zero, d_pre[:8]], 0)
    d_conv = below[3 : 3 + rows] * taps_ref[0:1, :]
    edge = above[8:16] * taps_ref[0:1, :]
    terms = [jnp.sum(d_pre * ext[5 : 5 + rows], 0, keepdims=True)]
    for j in range(1, CONV):
        d_conv = d_conv + below[3 - j : 3 - j + rows] * taps_ref[j : j + 1, :]
        edge = edge + above[8 - j : 16 - j] * taps_ref[j : j + 1, :]
        terms.append(jnp.sum(d_pre * ext[5 + j : 5 + j + rows], 0, keepdims=True))
    terms.append(jnp.sum(d_pre, 0, keepdims=True))
    return d_conv, edge, terms


def scan_bwd_kernel(conv_ref, conv_bc_ref, halo_ref, halo_bc_ref, taps_ref, taps_bc_ref, bias_ref, bias_bc_ref,
                    col_ref, row_ref, skip_ref, bc_ref, dy_ref, in_ref, out_ref,
                    dconv_ref, edge_ref, gt_ref, dconv_bc_ref, edge_bc_ref, gt_bc_ref, colo_ref, rowo_ref, misc_ref,
                    s_ref, ds_ref, dbc_ref):
    g = pl.program_id(0)
    rows = conv_ref.shape[0]

    @pl.when(g == 0)
    def _():
        s_ref[...] = masked_scores(bc_ref[:, N:], bc_ref[:, :N])
        ds_ref[...] = jnp.zeros_like(ds_ref)
        dbc_ref[...] = jnp.zeros_like(dbc_ref)

    ext = extend(halo_ref, conv_ref)
    pre = conv_pre(ext, taps_ref, bias_ref, rows)
    sig = sigmoid(pre)
    x = pre * sig
    low = lax.broadcasted_iota(jnp.int32, (rows, 2 * P_SIZE), 1) < P_SIZE
    lane = lax.broadcasted_iota(jnp.int32, (rows, 2 * K), 1)
    col = col_ref[0]
    row = row_ref[0]
    b_bf = bc_ref[:, :N].astype(BF)
    c_bf = bc_ref[:, N:].astype(BF)
    colo = jnp.zeros((rows, 2 * K), F32)
    dxs = []
    misc_ref[...] = jnp.zeros_like(misc_ref)
    rowo_ref[...] = jnp.zeros_like(rowo_ref)
    for pair in range(K // 2):
        h0 = 2 * pair
        cols = slice(pair * 128, pair * 128 + 128)
        x2 = x[:, cols]
        step = pair_cols(col, K + h0, low)
        xs = x2 * step
        xs_bf = xs.astype(BF)
        dy = dy_ref[:, cols]
        h_in = in_ref[cols, :]
        h_out = out_ref[cols, :]
        cum = pair_cols(col, h0, low)
        e = jnp.exp(cum)
        last = jnp.where(low[:1], row[h0 : h0 + 1, rows - 1 : rows], row[h0 + 1 : h0 + 2, rows - 1 : rows])
        tail = jnp.exp(last - cum)
        edy = e * dy
        txs = tail * xs
        inter = edy * mm_nt(c_bf, h_in)
        u = mm_nt(b_bf, h_out)
        r = txs * u
        dbc_ref[:, N:] += mm(edy, h_in)
        dbc_ref[:, :N] += mm(txs, h_out)
        d_xs = tail * u
        side = inter - r
        for i in range(2):
            h = h0 + i
            keep = low if i == 0 else ~low
            dyh = jnp.where(keep, dy, 0.0).astype(BF)
            d_mix = mm_nt(dyh, xs_bf)
            decay = jnp.exp(jnp.minimum(col[:, h : h + 1] - row[h : h + 1, :], 0.0))
            d_ld = d_mix * decay
            ds_ref[...] += d_ld
            s = s_ref[...]
            weight = d_ld * s
            d_xs = d_xs + mm_tn(s * decay, dyh)
            rowo_ref[0, h : h + 1, :] = jnp.sum(weight, 0, keepdims=True)
            folded = weight[:, :128] + weight[:, 128:] + jnp.where(keep, side, 0.0)
            colo = jnp.where(lane == h, jnp.sum(folded, 1, keepdims=True), colo)
        prod = x2 * d_xs
        for i in range(2):
            keep = low if i == 0 else ~low
            s_sum = jnp.sum(jnp.where(keep, prod, 0.0), 1, keepdims=True)
            colo = jnp.where(lane == K + h0 + i, s_sum, colo)
        dxs.append(step * d_xs + skip_ref[:, cols] * dy)
        hg = h_in.astype(F32) * h_out.astype(F32)
        misc_ref[0, 0:1, cols] = jnp.sum(dy * x2, 0, keepdims=True)
        misc_ref[0, 1:2, cols] = jnp.sum(r, 0, keepdims=True)
        misc_ref[0, 2:3, cols] = jnp.sum(hg[:P_SIZE], 0, keepdims=True)
        misc_ref[0, 3:4, cols] = jnp.sum(hg[P_SIZE:], 0, keepdims=True)
    colo_ref[0] = colo
    d_conv, edge, terms = conv_back(jnp.concatenate(dxs, 1), pre, sig, ext, taps_ref, rows)
    dconv_ref[...] = d_conv
    edge_ref[...] = edge
    gt_ref[...] = jnp.zeros_like(gt_ref)
    for j, term in enumerate(terms):
        gt_ref[j : j + 1, :] = term

    @pl.when(g == G - 1)
    def _():
        r_i = lax.broadcasted_iota(jnp.int32, ds_ref.shape, 0)
        q_i = lax.broadcasted_iota(jnp.int32, ds_ref.shape, 1)
        ds = jnp.where(r_i >= q_i, ds_ref[...], 0.0).astype(BF)
        d_c = dbc_ref[:, N:] + mm(ds, b_bf)
        d_b = dbc_ref[:, :N] + mm_tn(ds, c_bf)
        ext2 = extend(halo_bc_ref, conv_bc_ref)
        pre2 = conv_pre(ext2, taps_bc_ref, bias_bc_ref, rows)
        d_conv2, edge2, terms2 = conv_back(
            jnp.concatenate([d_b, d_c], 1), pre2, sigmoid(pre2), ext2, taps_bc_ref, rows)
        dconv_bc_ref[...] = d_conv2
        edge_bc_ref[...] = edge2
        gt_bc_ref[...] = jnp.zeros_like(gt_bc_ref)
        for j, term in enumerate(terms2):
            gt_bc_ref[j : j + 1, :] = term


def col_block(rows):
    return pl.BlockSpec((rows, W), lambda g: (0, g))


def bc_block(rows):
    return pl.BlockSpec((rows, W), lambda g: (0, G))


def fixed(shape):
    return pl.BlockSpec(shape, lambda g: (0,) * len(shape))


def packs(rows):
    return [pl.BlockSpec((1, rows, 2 * K), lambda g: (g, 0, 0)), pl.BlockSpec((1, 2 * K, rows), lambda g: (g, 0, 0))]


def conv_specs(rows):
    return [col_block(rows), bc_block(rows), col_block(8), bc_block(8), col_block(CONV), bc_block(CONV),
            col_block(1), bc_block(1)] + packs(rows) + [col_block(1)]


STATE = pl.BlockSpec((W, N), lambda g: (g, 0))


def sds(shape, dtype=F32):
    return jax.ShapeDtypeStruct(shape, dtype)


def scan_fwd(conv_in, halo, taps, bias, col, row, skip):
    rows = conv_in.shape[0]
    return pl.pallas_call(
        scan_fwd_kernel,
        grid=(G,),
        in_specs=conv_specs(rows),
        out_specs=[col_block(rows), STATE, fixed((rows, 2 * N))],
        out_shape=[sds((rows, DI)), sds((DI, N)), sds((rows, 2 * N))],
        scratch_shapes=[pltpu.VMEM((rows, rows), F32)],
        name="scan_fwd",
    )(conv_in, conv_in, halo, halo, taps, taps, bias, bias, col, row, skip)


def gate_fwd(y, gate, incoming, bc, col, gain):
    rows = y.shape[0]
    return pl.pallas_call(
        gate_fwd_kernel,
        grid=(G,),
        in_specs=[col_block(rows), col_block(rows), STATE, fixed((rows, 2 * N)), packs(rows)[0], fixed((1, DI))],
        out_specs=[col_block(rows), fixed((rows, DI))],
        out_shape=[sds((rows, DI)), sds((rows, DI), BF)],
        scratch_shapes=[pltpu.VMEM((G, rows, W), F32), pltpu.VMEM((rows, W), F32)],
        name="gate_fwd",
    )(y, gate, incoming, bc, col, gain)


def gate_bwd(ssm, gate, dn, gain, col, bc):
    rows = ssm.shape[0]
    block = pl.BlockSpec((rows, W), lambda p, g: (0, g))
    late = pl.BlockSpec((rows, W), lambda p, g: (0, p * g))
    return pl.pallas_call(
        gate_bwd_kernel,
        grid=(2, G),
        in_specs=[block, block, block, pl.BlockSpec((1, W), lambda p, g: (0, g)),
                  pl.BlockSpec((1, rows, 2 * K), lambda p, g: (g, 0, 0)),
                  pl.BlockSpec((rows, 2 * N), lambda p, g: (0, 0))],
        out_specs=[late, late, pl.BlockSpec((1, W), lambda p, g: (0, p * g)),
                   pl.BlockSpec((W, N), lambda p, g: (p * g, 0))],
        out_shape=[sds((rows, DI)), sds((rows, DI), BF), sds((1, DI)), sds((DI, N))],
        scratch_shapes=[pltpu.VMEM((rows, W), F32), pltpu.VMEM((rows, W), F32),
                        pltpu.VMEM((rows, 1), F32), pltpu.VMEM((rows, 1), F32)],
        name="gate_bwd",
    )(ssm, gate, dn, gain, col, bc)


def scan_bwd(conv_in, halo, taps, bias, col, row, skip, bc, dy, incoming, outgoing):
    rows = conv_in.shape[0]
    return pl.pallas_call(
        scan_bwd_kernel,
        grid=(G,),
        in_specs=conv_specs(rows) + [fixed((rows, 2 * N)), col_block(rows), STATE, STATE],
        out_specs=[col_block(rows), col_block(8), col_block(8), fixed((rows, W)), fixed((8, W)), fixed((8, W))]
        + packs(rows) + [pl.BlockSpec((1, 8, W), lambda g: (g, 0, 0))],
        out_shape=[sds((rows, DI)), sds((8, DI)), sds((8, DI)), sds((rows, W)), sds((8, W)), sds((8, W)),
                   sds((G, rows, 2 * K)), sds((G, 2 * K, rows)), sds((G, 8, W))],
        scratch_shapes=[pltpu.VMEM((rows, rows), F32), pltpu.VMEM((rows, rows), F32), pltpu.VMEM((rows, 2 * N), F32)],
        name="scan_bwd",
    )(conv_in, conv_in, halo, halo, taps, taps, bias, bias, col, row, skip, bc, dy, incoming, outgoing)


def passed_along(value, axis, steps):
    count = lax.axis_size(axis)
    initial, last = (max(0, -steps), min(count, count - steps))
    return lax.ppermute(value, axis, [(source, source + steps) for source in range(initial, last)])


CHUNKS = 2


def carry(totals, local_state, steps):
    hops = lax.axis_size("ctx") - 1
    size = DI // CHUNKS
    parts = []
    for chunk in range(CHUNKS):
        rows = slice(chunk * size, chunk * size + size)
        own, factor = local_state[rows], totals[rows]
        incoming = passed_along(own.astype(BF), "ctx", steps)
        for _ in range(hops - 1):
            incoming = passed_along((factor * incoming.astype(F32) + own).astype(BF), "ctx", steps)
        parts.append(incoming)
    return jnp.concatenate(parts, 0)


def all_sum(value):
    for axis in ("fsdp", "ctx"):
        count = lax.axis_size(axis)
        if count & (count - 1):
            value = lax.psum(value, axis)
            continue
        bit = 1
        while bit < count:
            value = value + lax.ppermute(value, axis, [(i, i ^ bit) for i in range(count)])
            bit *= 2
    return value


def rms_norm(values, gain_row):
    return values * lax.rsqrt(jnp.mean(values * values, axis=-1, keepdims=True) + EPS) * gain_row


def rows_product(left, right):
    return lax.dot_general(left, right, (((0,), (0,)), ((), ())), preferred_element_type=F32)


def right_transposed(left, right):
    return lax.dot_general(left, right, (((1,), (1,)), ((), ())), preferred_element_type=F32)


def gathered(value):
    return lax.all_gather(value, "fsdp", axis=0, tiled=True)


def to_owners(split):
    moved = lax.all_to_all(jnp.transpose(split, (1, 0, 2)), "fsdp", split_axis=0, concat_axis=0, tiled=True)
    return moved.reshape(-1, split.shape[2])


def by_run(part):
    fsdp_count, ctx_count = lax.axis_size("fsdp"), lax.axis_size("ctx")
    rows, width = part.shape
    own = rows // (fsdp_count * ctx_count)
    blocks = part.astype(BF).reshape(fsdp_count, ctx_count, own, width)
    return jnp.transpose(blocks, (1, 0, 2, 3)).reshape(ctx_count, fsdp_count * own, width)


def run_sum(blocks):
    flat = blocks.reshape(-1, blocks.shape[2])
    return lax.psum_scatter(flat, "ctx", scatter_dimension=0, tiled=True)


def early_gradients(normed_all, grad_all, d_gate, gnormed):
    fsdp_count, ctx_count = lax.axis_size("fsdp"), lax.axis_size("ctx")
    rows = d_gate.shape[0]
    width = DI // fsdp_count
    gate_cols = to_owners(d_gate.reshape(rows, fsdp_count, width))
    norm_cols = to_owners(gnormed.reshape(rows, fsdp_count, width))
    part_gate = by_run(rows_product(normed_all, gate_cols))
    part_out = rows_product(norm_cols, grad_all).astype(BF)
    tile = width // ctx_count
    model = part_out.shape[1]
    part_out = jnp.transpose(part_out.reshape(ctx_count, tile, model // width, width), (0, 2, 1, 3))
    part_out = part_out.reshape(ctx_count, -1, width)
    summed = run_sum(jnp.concatenate([part_gate, part_out], 1))
    in_rows = part_gate.shape[1]
    owned_out = jnp.transpose(summed[in_rows:].reshape(model // width, tile, width), (1, 0, 2))
    return summed[:in_rows], owned_out.reshape(tile, model).astype(F32)


def late_gradients(normed_all, d_x, d_small, gate_sum):
    fsdp_count = lax.axis_size("fsdp")
    rows = d_x.shape[0]
    width, extra = DI // fsdp_count, d_small.shape[1] // fsdp_count
    split = jnp.concatenate([d_x.reshape(rows, fsdp_count, width), d_small.reshape(rows, fsdp_count, extra)], 2)
    split = jnp.pad(split, ((0, 0), (0, 0), (0, -(width + extra) % 128)))
    part = rows_product(normed_all, to_owners(split))[:, : width + extra]
    rest_sum = run_sum(by_run(part))
    both = jnp.concatenate([gate_sum, rest_sum], 1)
    both = both.reshape(fsdp_count, -1, both.shape[1])
    both = lax.all_to_all(both, "fsdp", split_axis=0, concat_axis=0, tiled=True)
    both = jnp.transpose(both, (1, 0, 2))
    own = both.shape[0]
    parts = (both[:, :, :width], both[:, :, width : 2 * width], both[:, :, 2 * width :])
    return jnp.concatenate([part.reshape(own, -1) for part in parts], 1).astype(F32)


def grouped(cum, steps):
    rows = cum.shape[0]
    both = jnp.stack([cum.reshape(rows, G, K), steps.reshape(rows, G, K)], 2).reshape(rows, G, 2 * K)
    return jnp.transpose(both, (1, 0, 2)), jnp.transpose(both, (1, 2, 0))


def local(
    activations,
    in_weight,
    out_weight,
    norm_gain,
    conv_weight,
    conv_bias,
    step_bias,
    decay_log,
    skip_gain,
    gate_gain,
    cotangent,
):
    rows = activations.shape[0]
    edge_count = CONV - 1
    order = jnp.arange(rows)
    lower = (order[:, None] >= order[None, :]).astype(F32)
    in_rows = in_weight.shape[1]
    model = out_weight.shape[2]

    def side_by_side(k):
        return jnp.concatenate([out_weight[k, :in_rows], out_weight[k, in_rows:]], 1)

    def stacked_rows(full):
        blocks = jnp.transpose(full.reshape(-1, in_rows, 2, model), (0, 2, 1, 3))
        return blocks.reshape(DI, model)

    first = gathered(in_weight[0])
    middle = gathered(jnp.concatenate([side_by_side(0), in_weight[1, :, DI:]], 1))
    last = gathered(jnp.concatenate([in_weight[1, :, :DI], side_by_side(1)], 1))
    weights = [
        (first[:, DI:], first[:, :DI], stacked_rows(middle[:, :DI])),
        (middle[:, DI:], last[:, :DI], stacked_rows(last[:, DI:])),
    ]
    stream = activations
    kept = []
    for k in range(LAYERS):
        w_conv, w_gate, w_out = weights[k]
        normed = rms_norm(stream, norm_gain[k]).astype(BF)
        proj = jnp.dot(normed, w_conv, preferred_element_type=F32)
        conv_in = proj[:, :CC].astype(BF)
        raw_steps = proj[:, CC:]
        edge_in = passed_along(conv_in[rows - edge_count :], "ctx", 1)
        halo = jnp.concatenate([jnp.zeros((8 - edge_count, CC), F32), edge_in.astype(F32)], 0)
        steps = jax.nn.softplus(raw_steps + step_bias[k][None, :])
        cum = jnp.dot(lower, -steps * jnp.exp(decay_log[k])[None, :], precision=HIGH)
        col, row = grouped(cum, steps)
        totals = jnp.repeat(jnp.exp(cum[-1]), P_SIZE)[:, None]
        skip = jnp.repeat(skip_gain[k], P_SIZE)[None, :]
        bias = conv_bias[k][None, :]
        y, state, bc = scan_fwd(conv_in, halo, conv_weight[k], bias, col, row, skip)
        gate_in = jnp.dot(normed, w_gate, preferred_element_type=F32)
        incoming = carry(totals, state, 1)
        ssm, gnormed = gate_fwd(y, gate_in, incoming, bc, col, gate_gain[k][None, :])
        kept.append((stream, normed, gate_in, conv_in, halo, raw_steps, steps, col, row, totals, skip, bias, bc,
                     incoming, ssm, gnormed))
        stream = stream + jnp.dot(gnormed, w_out, preferred_element_type=F32)
    grad_stream = cotangent
    token_rows = gathered(jnp.concatenate([kept[0][1], kept[1][1], cotangent.astype(BF)], 1))
    collected = []
    for k in reversed(range(LAYERS)):
        w_conv, w_gate, w_out = weights[k]
        (stream_in, normed, gate_in, conv_in, halo, raw_steps, steps, col, row, totals, skip, bias, bc,
         incoming, ssm, gnormed) = kept[k]
        grad_bf = grad_stream.astype(BF)
        d_gnormed = right_transposed(grad_bf, w_out)
        d_ssm, d_gate, g_gate, local_grad = gate_bwd(ssm, gate_in, d_gnormed, gate_gain[k][None, :], col, bc)
        outgoing = carry(totals, local_grad, -1)
        normed_all = token_rows[:, k * model : (k + 1) * model]
        grad_all = token_rows[:, LAYERS * model :] if k == LAYERS - 1 else gathered(grad_bf)
        gate_sum, owned_out = early_gradients(normed_all, grad_all, d_gate, gnormed)
        d_x, edge_x, gt_x, d_bc, edge_bc, gt_bc, colo, rowo, misc = scan_bwd(
            conv_in, halo, conv_weight[k], bias, col, row, skip, bc, d_ssm, incoming, outgoing)
        edges = jnp.concatenate([edge_x[:edge_count], edge_bc[:edge_count]], 1)
        edge_back = passed_along(edges, "ctx", -1)
        taps_grad = jnp.concatenate([gt_x, gt_bc], 1)
        colf = jnp.transpose(colo, (1, 0, 2))
        d_cum = colf[:, :, :K].reshape(rows, H) - jnp.transpose(rowo[:, :K], (2, 0, 1)).reshape(rows, H)
        g_skip = misc[:, 0].reshape(H, P_SIZE).sum(1)
        r_sum = misc[:, 1].reshape(H, P_SIZE).sum(1)
        hg = jnp.transpose(misc[:, 2:4].reshape(G, 2, 2, N), (0, 2, 1, 3)).sum(-1).reshape(H)
        d_last = r_sum + totals[::P_SIZE, 0] * hg
        d_cum = d_cum + jnp.where(order[:, None] == rows - 1, d_last[None, :], 0.0)
        d_log = jnp.dot(lower.T, d_cum, precision=HIGH)
        rate = jnp.exp(decay_log[k])[None, :]
        d_step = colf[:, :, K:].reshape(rows, H) - d_log * rate
        d_raw = d_step * jax.nn.sigmoid(raw_steps + step_bias[k][None, :])
        g_bias = d_raw.sum(0)
        g_log = -(d_log * steps * rate).sum(0)
        d_conv = jnp.concatenate([d_x, d_bc], 1)
        d_conv = d_conv + jnp.pad(edge_back, ((rows - edge_count, 0), (0, 0)))
        d_rest = jnp.concatenate([d_conv, d_raw], 1).astype(BF)
        d_normed = right_transposed(d_gate, w_gate) + right_transposed(d_rest, w_conv)
        _, pullback = jax.vjp(rms_norm, stream_in, norm_gain[k])
        d_stream, g_norm = pullback(d_normed)
        grad_stream = grad_stream + d_stream
        owned_in = late_gradients(normed_all, d_rest[:, :DI], d_rest[:, DI:], gate_sum)
        small = [g_norm, taps_grad[:CONV].reshape(-1), taps_grad[CONV], g_bias, g_log, g_skip, g_gate.reshape(-1)]
        sizes = [part.shape[0] for part in small]
        flat = jnp.concatenate(small)
        flat = all_sum(jnp.pad(flat, (0, -flat.shape[0] % 1024)).reshape(-1, 128)).reshape(-1)
        parts, at = [], 0
        for size in sizes:
            parts.append(flat[at : at + size])
            at += size
        parts[1] = parts[1].reshape(CONV, CC)
        collected.append((owned_in, owned_out, *parts))
    collected = collected[::-1]
    stacked = [jnp.stack([entry[member] for entry in collected], 0) for member in range(9)]
    return (stream, grad_stream, *stacked)


def solution(mesh):
    tokens = P(("fsdp", "ctx"), None)
    sharded = P(None, "fsdp", None)
    owned = P(None, ("fsdp", "ctx"), None)
    return jax.shard_map(
        local,
        mesh=mesh,
        in_specs=(tokens, sharded, sharded) + (P(),) * 7 + (tokens,),
        out_specs=(tokens, tokens, owned, owned) + (P(),) * 7,
        check_vma=False,
    )
```

```python
import functools

import jax
import jax.numpy as jnp
from jax import lax
from jax.experimental import pallas as pl
from jax.experimental.pallas import tpu as pltpu
from jax.sharding import PartitionSpec as P

H = 48
P_SIZE = 64
N = 128
CONV = 4
LAYERS = 2
DI = 3072
CC = 3328
W = 256
G = DI // W
K = W // P_SIZE

EPS = 1e-05
HIGH = lax.Precision.HIGHEST
F32 = jnp.float32
BF = jnp.bfloat16


def mm(a, b):
    return lax.dot_general(a.astype(BF), b.astype(BF), (((1,), (0,)), ((), ())), preferred_element_type=F32)


def mm_nt(a, b):
    return lax.dot_general(a.astype(BF), b.astype(BF), (((1,), (1,)), ((), ())), preferred_element_type=F32)


def mm_tn(a, b):
    return lax.dot_general(a.astype(BF), b.astype(BF), (((0,), (0,)), ((), ())), preferred_element_type=F32)


def extend(halo_ref, conv_ref):
    return jnp.concatenate([halo_ref[...], conv_ref[...].astype(F32)], 0)


def conv_pre(ext, taps_ref, bias_ref, rows):
    acc = bias_ref[...] + ext[5 : 5 + rows] * taps_ref[0:1, :]
    for j in range(1, CONV):
        acc = acc + ext[5 + j : 5 + j + rows] * taps_ref[j : j + 1, :]
    return acc


def sigmoid(v):
    return 1.0 / (1.0 + jnp.exp(-v))


def pair_cols(col, first, low):
    return jnp.where(low, col[:, first : first + 1], col[:, first + 1 : first + 2])


def masked_scores(c_rows, b_rows):
    s = mm_nt(c_rows, b_rows)
    r = lax.broadcasted_iota(jnp.int32, s.shape, 0)
    q = lax.broadcasted_iota(jnp.int32, s.shape, 1)
    return jnp.where(r >= q, s, 0.0)


def scan_fwd_kernel(conv_ref, conv_bc_ref, halo_ref, halo_bc_ref, taps_ref, taps_bc_ref, bias_ref, bias_bc_ref,
                    col_ref, row_ref, skip_ref, y_ref, state_ref, bc_ref, s_ref):
    rows = conv_ref.shape[0]

    @pl.when(pl.program_id(0) == 0)
    def _():
        pre = conv_pre(extend(halo_bc_ref, conv_bc_ref), taps_bc_ref, bias_bc_ref, rows)
        bc = pre * sigmoid(pre)
        bc_ref[...] = bc
        s_ref[...] = masked_scores(bc[:, N:], bc[:, :N])

    pre = conv_pre(extend(halo_ref, conv_ref), taps_ref, bias_ref, rows)
    x = pre * sigmoid(pre)
    low = lax.broadcasted_iota(jnp.int32, (rows, 2 * P_SIZE), 1) < P_SIZE
    col = col_ref[0]
    row = row_ref[0]
    b_bf = bc_ref[:, :N].astype(BF)
    for pair in range(K // 2):
        h0 = 2 * pair
        cols = slice(pair * 128, pair * 128 + 128)
        x2 = x[:, cols]
        xs = x2 * pair_cols(col, K + h0, low)
        mixes, parts = [], []
        for i in range(2):
            h = h0 + i
            decay = jnp.exp(jnp.minimum(col[:, h : h + 1] - row[h : h + 1, :], 0.0))
            mixes.append((s_ref[...] * decay).astype(BF))
            parts.append(jnp.where(low if i == 0 else ~low, xs, 0.0).astype(BF))
        y = mm(jnp.concatenate(mixes, 1), jnp.concatenate(parts, 0))
        y_ref[:, cols] = y + skip_ref[:, cols] * x2
        last = jnp.where(low[:1], row[h0 : h0 + 1, rows - 1 : rows], row[h0 + 1 : h0 + 2, rows - 1 : rows])
        tail = jnp.exp(last - pair_cols(col, h0, low))
        state_ref[cols, :] = mm_tn(xs * tail, b_bf)


def gate_fwd_kernel(y_ref, gate_ref, in_ref, bc_ref, col_ref, gain_ref, ssm_ref, gn_ref, gated_ref, acc_ref):
    g = pl.program_id(0)
    rows = y_ref.shape[0]

    @pl.when(g == 0)
    def _():
        acc_ref[...] = jnp.zeros_like(acc_ref)

    low = lax.broadcasted_iota(jnp.int32, (rows, 2 * P_SIZE), 1) < P_SIZE
    col = col_ref[0]
    z = mm_nt(bc_ref[:, N:], in_ref[...])
    e = jnp.concatenate([jnp.exp(pair_cols(col, 2 * p, low)) for p in range(K // 2)], 1)
    ssm = y_ref[...] + e * z
    ssm_ref[...] = ssm
    gate = gate_ref[...]
    gated = ssm * (gate * sigmoid(gate))
    gated_ref[g] = gated
    acc_ref[...] += gated * gated

    @pl.when(g == G - 1)
    def _():
        r = lax.rsqrt(jnp.sum(acc_ref[...], 1, keepdims=True) / DI + EPS)
        for i in range(G):
            cols = slice(i * W, i * W + W)
            gn_ref[:, cols] = (gated_ref[i] * r * gain_ref[:, cols]).astype(BF)


def gate_bwd_kernel(ssm_ref, gate_ref, dn_ref, gain_ref, col_ref, bc_ref, dssm_ref, dgate_ref, ggain_ref, lg_ref,
                    sq_ref, dot_ref, r_ref, k_ref):
    phase = pl.program_id(0)
    g = pl.program_id(1)
    rows = ssm_ref.shape[0]
    ssm = ssm_ref[...]
    gate = gate_ref[...]
    sig = sigmoid(gate)
    act = gate * sig
    gated = ssm * act
    dn = dn_ref[...]
    dng = dn * gain_ref[...]

    @pl.when((phase == 0) & (g == 0))
    def _():
        sq_ref[...] = jnp.zeros_like(sq_ref)
        dot_ref[...] = jnp.zeros_like(dot_ref)

    @pl.when(phase == 0)
    def _():
        sq_ref[...] += gated * gated
        dot_ref[...] += dng * gated

    @pl.when((phase == 1) & (g == 0))
    def _():
        r = lax.rsqrt(jnp.sum(sq_ref[...], 1, keepdims=True) / DI + EPS)
        r_ref[...] = r
        k_ref[...] = r * r * r * jnp.sum(dot_ref[...], 1, keepdims=True) / DI

    @pl.when(phase == 1)
    def _():
        r = r_ref[...]
        dgated = r * dng - gated * k_ref[...]
        dssm = dgated * act
        dssm_ref[...] = dssm
        dgate_ref[...] = (dgated * ssm * (sig * (1.0 + gate * (1.0 - sig)))).astype(BF)
        ggain_ref[...] = jnp.sum(dn * (gated * r), 0, keepdims=True)
        low = lax.broadcasted_iota(jnp.int32, (rows, 2 * P_SIZE), 1) < P_SIZE
        col = col_ref[0]
        e = jnp.concatenate([jnp.exp(pair_cols(col, 2 * p, low)) for p in range(K // 2)], 1)
        lg_ref[...] = mm_tn(dssm * e, bc_ref[:, N:])


def conv_back(d_act, pre, sig, ext, taps_ref, rows):
    d_pre = d_act * (sig * (1.0 + pre * (1.0 - sig)))
    zero = jnp.zeros((8, d_pre.shape[1]), F32)
    below = jnp.concatenate([d_pre, zero], 0)
    above = jnp.concatenate([zero, d_pre[:8]], 0)
    d_conv = below[3 : 3 + rows] * taps_ref[0:1, :]
    edge = above[8:16] * taps_ref[0:1, :]
    terms = [jnp.sum(d_pre * ext[5 : 5 + rows], 0, keepdims=True)]
    for j in range(1, CONV):
        d_conv = d_conv + below[3 - j : 3 - j + rows] * taps_ref[j : j + 1, :]
        edge = edge + above[8 - j : 16 - j] * taps_ref[j : j + 1, :]
        terms.append(jnp.sum(d_pre * ext[5 + j : 5 + j + rows], 0, keepdims=True))
    terms.append(jnp.sum(d_pre, 0, keepdims=True))
    return d_conv, edge, terms


def scan_bwd_kernel(conv_ref, conv_bc_ref, halo_ref, halo_bc_ref, taps_ref, taps_bc_ref, bias_ref, bias_bc_ref,
                    col_ref, row_ref, skip_ref, bc_ref, dy_ref, in_ref, out_ref,
                    dconv_ref, edge_ref, gt_ref, dconv_bc_ref, edge_bc_ref, gt_bc_ref, colo_ref, rowo_ref, misc_ref,
                    s_ref, ds_ref, dbc_ref):
    g = pl.program_id(0)
    rows = conv_ref.shape[0]

    @pl.when(g == 0)
    def _():
        s_ref[...] = masked_scores(bc_ref[:, N:], bc_ref[:, :N])
        ds_ref[...] = jnp.zeros_like(ds_ref)
        dbc_ref[...] = jnp.zeros_like(dbc_ref)

    ext = extend(halo_ref, conv_ref)
    pre = conv_pre(ext, taps_ref, bias_ref, rows)
    sig = sigmoid(pre)
    x = pre * sig
    low = lax.broadcasted_iota(jnp.int32, (rows, 2 * P_SIZE), 1) < P_SIZE
    lane = lax.broadcasted_iota(jnp.int32, (rows, 2 * K), 1)
    col = col_ref[0]
    row = row_ref[0]
    b_bf = bc_ref[:, :N].astype(BF)
    c_bf = bc_ref[:, N:].astype(BF)
    colo = jnp.zeros((rows, 2 * K), F32)
    dxs = []
    misc_ref[...] = jnp.zeros_like(misc_ref)
    rowo_ref[...] = jnp.zeros_like(rowo_ref)
    for pair in range(K // 2):
        h0 = 2 * pair
        cols = slice(pair * 128, pair * 128 + 128)
        x2 = x[:, cols]
        step = pair_cols(col, K + h0, low)
        xs = x2 * step
        xs_bf = xs.astype(BF)
        dy = dy_ref[:, cols]
        h_in = in_ref[cols, :]
        h_out = out_ref[cols, :]
        cum = pair_cols(col, h0, low)
        e = jnp.exp(cum)
        last = jnp.where(low[:1], row[h0 : h0 + 1, rows - 1 : rows], row[h0 + 1 : h0 + 2, rows - 1 : rows])
        tail = jnp.exp(last - cum)
        edy = e * dy
        txs = tail * xs
        inter = edy * mm_nt(c_bf, h_in)
        u = mm_nt(b_bf, h_out)
        r = txs * u
        dbc_ref[:, N:] += mm(edy, h_in)
        dbc_ref[:, :N] += mm(txs, h_out)
        d_xs = tail * u
        side = inter - r
        for i in range(2):
            h = h0 + i
            keep = low if i == 0 else ~low
            dyh = jnp.where(keep, dy, 0.0).astype(BF)
            d_mix = mm_nt(dyh, xs_bf)
            decay = jnp.exp(jnp.minimum(col[:, h : h + 1] - row[h : h + 1, :], 0.0))
            d_ld = d_mix * decay
            ds_ref[...] += d_ld
            s = s_ref[...]
            weight = d_ld * s
            d_xs = d_xs + mm_tn(s * decay, dyh)
            rowo_ref[0, h : h + 1, :] = jnp.sum(weight, 0, keepdims=True)
            folded = weight[:, :128] + weight[:, 128:] + jnp.where(keep, side, 0.0)
            colo = jnp.where(lane == h, jnp.sum(folded, 1, keepdims=True), colo)
        prod = x2 * d_xs
        for i in range(2):
            keep = low if i == 0 else ~low
            s_sum = jnp.sum(jnp.where(keep, prod, 0.0), 1, keepdims=True)
            colo = jnp.where(lane == K + h0 + i, s_sum, colo)
        dxs.append(step * d_xs + skip_ref[:, cols] * dy)
        hg = h_in.astype(F32) * h_out.astype(F32)
        misc_ref[0, 0:1, cols] = jnp.sum(dy * x2, 0, keepdims=True)
        misc_ref[0, 1:2, cols] = jnp.sum(r, 0, keepdims=True)
        misc_ref[0, 2:3, cols] = jnp.sum(hg[:P_SIZE], 0, keepdims=True)
        misc_ref[0, 3:4, cols] = jnp.sum(hg[P_SIZE:], 0, keepdims=True)
    colo_ref[0] = colo
    d_conv, edge, terms = conv_back(jnp.concatenate(dxs, 1), pre, sig, ext, taps_ref, rows)
    dconv_ref[...] = d_conv
    edge_ref[...] = edge
    gt_ref[...] = jnp.zeros_like(gt_ref)
    for j, term in enumerate(terms):
        gt_ref[j : j + 1, :] = term

    @pl.when(g == G - 1)
    def _():
        r_i = lax.broadcasted_iota(jnp.int32, ds_ref.shape, 0)
        q_i = lax.broadcasted_iota(jnp.int32, ds_ref.shape, 1)
        ds = jnp.where(r_i >= q_i, ds_ref[...], 0.0).astype(BF)
        d_c = dbc_ref[:, N:] + mm(ds, b_bf)
        d_b = dbc_ref[:, :N] + mm_tn(ds, c_bf)
        ext2 = extend(halo_bc_ref, conv_bc_ref)
        pre2 = conv_pre(ext2, taps_bc_ref, bias_bc_ref, rows)
        d_conv2, edge2, terms2 = conv_back(
            jnp.concatenate([d_b, d_c], 1), pre2, sigmoid(pre2), ext2, taps_bc_ref, rows)
        dconv_bc_ref[...] = d_conv2
        edge_bc_ref[...] = edge2
        gt_bc_ref[...] = jnp.zeros_like(gt_bc_ref)
        for j, term in enumerate(terms2):
            gt_bc_ref[j : j + 1, :] = term


def col_block(rows):
    return pl.BlockSpec((rows, W), lambda g: (0, g))


def bc_block(rows):
    return pl.BlockSpec((rows, W), lambda g: (0, G))


def fixed(shape):
    return pl.BlockSpec(shape, lambda g: (0,) * len(shape))


def packs(rows):
    return [pl.BlockSpec((1, rows, 2 * K), lambda g: (g, 0, 0)), pl.BlockSpec((1, 2 * K, rows), lambda g: (g, 0, 0))]


def conv_specs(rows):
    return [col_block(rows), bc_block(rows), col_block(8), bc_block(8), col_block(CONV), bc_block(CONV),
            col_block(1), bc_block(1)] + packs(rows) + [col_block(1)]


STATE = pl.BlockSpec((W, N), lambda g: (g, 0))


def sds(shape, dtype=F32):
    return jax.ShapeDtypeStruct(shape, dtype)


def scan_fwd(conv_in, halo, taps, bias, col, row, skip):
    rows = conv_in.shape[0]
    return pl.pallas_call(
        scan_fwd_kernel,
        grid=(G,),
        in_specs=conv_specs(rows),
        out_specs=[col_block(rows), STATE, fixed((rows, 2 * N))],
        out_shape=[sds((rows, DI)), sds((DI, N)), sds((rows, 2 * N))],
        scratch_shapes=[pltpu.VMEM((rows, rows), F32)],
        name="scan_fwd",
    )(conv_in, conv_in, halo, halo, taps, taps, bias, bias, col, row, skip)


def gate_fwd(y, gate, incoming, bc, col, gain):
    rows = y.shape[0]
    return pl.pallas_call(
        gate_fwd_kernel,
        grid=(G,),
        in_specs=[col_block(rows), col_block(rows), STATE, fixed((rows, 2 * N)), packs(rows)[0], fixed((1, DI))],
        out_specs=[col_block(rows), fixed((rows, DI))],
        out_shape=[sds((rows, DI)), sds((rows, DI), BF)],
        scratch_shapes=[pltpu.VMEM((G, rows, W), F32), pltpu.VMEM((rows, W), F32)],
        name="gate_fwd",
    )(y, gate, incoming, bc, col, gain)


def gate_bwd(ssm, gate, dn, gain, col, bc):
    rows = ssm.shape[0]
    block = pl.BlockSpec((rows, W), lambda p, g: (0, g))
    late = pl.BlockSpec((rows, W), lambda p, g: (0, p * g))
    return pl.pallas_call(
        gate_bwd_kernel,
        grid=(2, G),
        in_specs=[block, block, block, pl.BlockSpec((1, W), lambda p, g: (0, g)),
                  pl.BlockSpec((1, rows, 2 * K), lambda p, g: (g, 0, 0)),
                  pl.BlockSpec((rows, 2 * N), lambda p, g: (0, 0))],
        out_specs=[late, late, pl.BlockSpec((1, W), lambda p, g: (0, p * g)),
                   pl.BlockSpec((W, N), lambda p, g: (p * g, 0))],
        out_shape=[sds((rows, DI)), sds((rows, DI), BF), sds((1, DI)), sds((DI, N))],
        scratch_shapes=[pltpu.VMEM((rows, W), F32), pltpu.VMEM((rows, W), F32),
                        pltpu.VMEM((rows, 1), F32), pltpu.VMEM((rows, 1), F32)],
        name="gate_bwd",
    )(ssm, gate, dn, gain, col, bc)


def scan_bwd(conv_in, halo, taps, bias, col, row, skip, bc, dy, incoming, outgoing):
    rows = conv_in.shape[0]
    return pl.pallas_call(
        scan_bwd_kernel,
        grid=(G,),
        in_specs=conv_specs(rows) + [fixed((rows, 2 * N)), col_block(rows), STATE, STATE],
        out_specs=[col_block(rows), col_block(8), col_block(8), fixed((rows, W)), fixed((8, W)), fixed((8, W))]
        + packs(rows) + [pl.BlockSpec((1, 8, W), lambda g: (g, 0, 0))],
        out_shape=[sds((rows, DI)), sds((8, DI)), sds((8, DI)), sds((rows, W)), sds((8, W)), sds((8, W)),
                   sds((G, rows, 2 * K)), sds((G, 2 * K, rows)), sds((G, 8, W))],
        scratch_shapes=[pltpu.VMEM((rows, rows), F32), pltpu.VMEM((rows, rows), F32), pltpu.VMEM((rows, 2 * N), F32)],
        name="scan_bwd",
    )(conv_in, conv_in, halo, halo, taps, taps, bias, bias, col, row, skip, bc, dy, incoming, outgoing)


def passed_along(value, axis, steps):
    count = lax.axis_size(axis)
    initial, last = (max(0, -steps), min(count, count - steps))
    return lax.ppermute(value, axis, [(source, source + steps) for source in range(initial, last)])


CHUNKS = 2


def carry(totals, local_state, steps):
    hops = lax.axis_size("ctx") - 1
    size = DI // CHUNKS
    parts = []
    for chunk in range(CHUNKS):
        rows = slice(chunk * size, chunk * size + size)
        own, factor = local_state[rows], totals[rows]
        incoming = passed_along(own.astype(BF), "ctx", steps)
        for _ in range(hops - 1):
            incoming = passed_along((factor * incoming.astype(F32) + own).astype(BF), "ctx", steps)
        parts.append(incoming)
    return jnp.concatenate(parts, 0)


def all_sum(value):
    for axis in ("fsdp", "ctx"):
        count = lax.axis_size(axis)
        if count & (count - 1):
            value = lax.psum(value, axis)
            continue
        bit = 1
        while bit < count:
            value = value + lax.ppermute(value, axis, [(i, i ^ bit) for i in range(count)])
            bit *= 2
    return value


def rms_norm(values, gain_row):
    return values * lax.rsqrt(jnp.mean(values * values, axis=-1, keepdims=True) + EPS) * gain_row


def rows_product(left, right):
    return lax.dot_general(left, right, (((0,), (0,)), ((), ())), preferred_element_type=F32)


def right_transposed(left, right):
    return lax.dot_general(left, right, (((1,), (1,)), ((), ())), preferred_element_type=F32)


def gathered(value):
    return lax.all_gather(value, "fsdp", axis=0, tiled=True)


def to_owners(split):
    moved = lax.all_to_all(jnp.transpose(split, (1, 0, 2)), "fsdp", split_axis=0, concat_axis=0, tiled=True)
    return moved.reshape(-1, split.shape[2])


def by_run(part):
    fsdp_count, ctx_count = lax.axis_size("fsdp"), lax.axis_size("ctx")
    rows, width = part.shape
    own = rows // (fsdp_count * ctx_count)
    blocks = part.astype(BF).reshape(fsdp_count, ctx_count, own, width)
    return jnp.transpose(blocks, (1, 0, 2, 3)).reshape(ctx_count, fsdp_count * own, width)


def run_sum(blocks):
    flat = blocks.reshape(-1, blocks.shape[2])
    return lax.psum_scatter(flat, "ctx", scatter_dimension=0, tiled=True)


def gate_parts(normed_all, d_gate):
    fsdp_count = lax.axis_size("fsdp")
    return by_run(rows_product(normed_all, to_owners(d_gate.reshape(d_gate.shape[0], fsdp_count, -1))))


def out_parts(norm_cols, grad_all):
    ctx_count = lax.axis_size("ctx")
    width, model = norm_cols.shape[1], grad_all.shape[1]
    part = rows_product(norm_cols, grad_all).astype(BF)
    part = part.reshape(ctx_count, width // ctx_count, model // width, width)
    return jnp.transpose(part, (0, 2, 1, 3)).reshape(ctx_count, -1, width)


def early_sum(part_gate, part_out, model):
    summed = run_sum(jnp.concatenate([part_gate, part_out], 1))
    in_rows, width = part_gate.shape[1:]
    owned_out = jnp.transpose(summed[in_rows:].reshape(model // width, -1, width), (1, 0, 2))
    return summed[:in_rows], owned_out.reshape(-1, model).astype(F32)


def rest_parts(normed_all, d_rest):
    fsdp_count = lax.axis_size("fsdp")
    rows = d_rest.shape[0]
    wide = d_rest[:, :DI].reshape(rows, fsdp_count, -1)
    narrow = d_rest[:, DI:].reshape(rows, fsdp_count, -1)
    width = wide.shape[2] + narrow.shape[2]
    split = jnp.concatenate([wide, narrow, jnp.zeros((rows, fsdp_count, -width % 128), BF)], 2)
    return by_run(rows_product(normed_all, to_owners(split))[:, :width])


def late_sum(part_rest, gate_sum):
    fsdp_count = lax.axis_size("fsdp")
    width = gate_sum.shape[1]
    both = jnp.concatenate([gate_sum, run_sum(part_rest)], 1)
    both = both.reshape(fsdp_count, -1, both.shape[1])
    both = lax.all_to_all(both, "fsdp", split_axis=0, concat_axis=0, tiled=True)
    both = jnp.transpose(both, (1, 0, 2))
    own = both.shape[0]
    parts = (both[:, :, :width], both[:, :, width : 2 * width], both[:, :, 2 * width :])
    return jnp.concatenate([part.reshape(own, -1) for part in parts], 1).astype(F32)


def grouped(cum, steps):
    rows = cum.shape[0]
    both = jnp.stack([cum.reshape(rows, G, K), steps.reshape(rows, G, K)], 2).reshape(rows, G, 2 * K)
    return jnp.transpose(both, (1, 0, 2)), jnp.transpose(both, (1, 2, 0))


def local(
    activations,
    in_weight,
    out_weight,
    norm_gain,
    conv_weight,
    conv_bias,
    step_bias,
    decay_log,
    skip_gain,
    gate_gain,
    cotangent,
):
    rows = activations.shape[0]
    edge_count = CONV - 1
    order = jnp.arange(rows)
    lower = (order[:, None] >= order[None, :]).astype(F32)
    model = out_weight.shape[2]
    first = gathered(in_weight[0])
    weights = [(first[:, DI:], first[:, :DI], gathered(out_weight[0]))]
    for k in range(1, LAYERS):
        weights.append((gathered(in_weight[k][:, DI:]), gathered(in_weight[k][:, :DI]), gathered(out_weight[k])))
    stream = activations
    kept = []
    for k in range(LAYERS):
        w_conv, w_gate, w_out = weights[k]
        normed = rms_norm(stream, norm_gain[k]).astype(BF)
        proj = jnp.dot(normed, w_conv, preferred_element_type=F32)
        conv_in = proj[:, :CC].astype(BF)
        raw_steps = proj[:, CC:]
        edge_in = passed_along(conv_in[rows - edge_count :], "ctx", 1)
        halo = jnp.concatenate([jnp.zeros((8 - edge_count, CC), F32), edge_in.astype(F32)], 0)
        steps = jax.nn.softplus(raw_steps + step_bias[k][None, :])
        cum = jnp.dot(lower, -steps * jnp.exp(decay_log[k])[None, :], precision=HIGH)
        col, row = grouped(cum, steps)
        totals = jnp.repeat(jnp.exp(cum[-1]), P_SIZE)[:, None]
        skip = jnp.repeat(skip_gain[k], P_SIZE)[None, :]
        bias = conv_bias[k][None, :]
        y, state, bc = scan_fwd(conv_in, halo, conv_weight[k], bias, col, row, skip)
        gate_in = jnp.dot(normed, w_gate, preferred_element_type=F32)
        incoming = carry(totals, state, 1)
        ssm, gnormed = gate_fwd(y, gate_in, incoming, bc, col, gate_gain[k][None, :])
        kept.append((stream, normed, gate_in, conv_in, halo, raw_steps, steps, col, row, totals, skip, bias, bc,
                     incoming, ssm, gnormed))
        stream = stream + jnp.dot(gnormed, w_out, preferred_element_type=F32)
    grad_stream = cotangent
    token_rows = gathered(jnp.concatenate([kept[0][1], kept[1][1], cotangent.astype(BF)], 1))
    width = DI // lax.axis_size("fsdp")
    norm_cols = to_owners(jnp.concatenate([kept[k][-1].reshape(rows, -1, width) for k in range(LAYERS)], 2))
    norm_cols = [norm_cols[:, k * width : (k + 1) * width] for k in range(LAYERS)]
    collected, owned_ins, waiting = [], [], None
    for k in reversed(range(LAYERS)):
        w_conv, w_gate, w_out = weights[k]
        (stream_in, normed, gate_in, conv_in, halo, raw_steps, steps, col, row, totals, skip, bias, bc,
         incoming, ssm, gnormed) = kept[k]
        grad_bf = grad_stream.astype(BF)
        d_gnormed = right_transposed(grad_bf, w_out)
        d_ssm, d_gate, g_gate, local_grad = gate_bwd(ssm, gate_in, d_gnormed, gate_gain[k][None, :], col, bc)
        outgoing = carry(totals, local_grad, -1)
        normed_all = token_rows[:, k * model : (k + 1) * model]
        grad_all = token_rows[:, LAYERS * model :] if k == LAYERS - 1 else gathered(grad_bf)
        part_gate = gate_parts(normed_all, d_gate)
        part_out = out_parts(norm_cols[k], grad_all)
        if waiting is None:
            outgoing, part_gate, part_out, norm_cols = lax.optimization_barrier(
                (outgoing, part_gate, part_out, norm_cols))
        else:
            outgoing, part_gate, part_out, part_rest = lax.optimization_barrier(
                (outgoing, part_gate, part_out, waiting[0]))
            owned_ins.append(late_sum(part_rest, waiting[1]))
        gate_sum, owned_out = early_sum(part_gate, part_out, model)
        d_x, edge_x, gt_x, d_bc, edge_bc, gt_bc, colo, rowo, misc = scan_bwd(
            conv_in, halo, conv_weight[k], bias, col, row, skip, bc, d_ssm, incoming, outgoing)
        edges = jnp.concatenate([edge_x[:edge_count], edge_bc[:edge_count]], 1)
        edge_back = passed_along(edges, "ctx", -1)
        taps_grad = jnp.concatenate([gt_x, gt_bc], 1)
        colf = jnp.transpose(colo, (1, 0, 2))
        d_cum = colf[:, :, :K].reshape(rows, H) - jnp.transpose(rowo[:, :K], (2, 0, 1)).reshape(rows, H)
        g_skip = misc[:, 0].reshape(H, P_SIZE).sum(1)
        r_sum = misc[:, 1].reshape(H, P_SIZE).sum(1)
        hg = jnp.transpose(misc[:, 2:4].reshape(G, 2, 2, N), (0, 2, 1, 3)).sum(-1).reshape(H)
        d_last = r_sum + totals[::P_SIZE, 0] * hg
        d_cum = d_cum + jnp.where(order[:, None] == rows - 1, d_last[None, :], 0.0)
        d_log = jnp.dot(lower.T, d_cum, precision=HIGH)
        rate = jnp.exp(decay_log[k])[None, :]
        d_step = colf[:, :, K:].reshape(rows, H) - d_log * rate
        d_raw = d_step * jax.nn.sigmoid(raw_steps + step_bias[k][None, :])
        g_bias = d_raw.sum(0)
        g_log = -(d_log * steps * rate).sum(0)
        d_conv = jnp.concatenate([d_x, d_bc], 1)
        d_conv = d_conv + jnp.pad(edge_back, ((rows - edge_count, 0), (0, 0)))
        d_rest = jnp.concatenate([d_conv, d_raw], 1).astype(BF)
        d_normed = right_transposed(d_gate, w_gate) + right_transposed(d_rest, w_conv)
        _, pullback = jax.vjp(rms_norm, stream_in, norm_gain[k])
        d_stream, g_norm = pullback(d_normed)
        grad_stream = grad_stream + d_stream
        waiting = (rest_parts(normed_all, d_rest), gate_sum)
        small = [g_norm, taps_grad[:CONV].reshape(-1), taps_grad[CONV], g_bias, g_log, g_skip, g_gate.reshape(-1)]
        sizes = [part.shape[0] for part in small]
        flat = jnp.concatenate(small)
        flat = all_sum(jnp.pad(flat, (0, -flat.shape[0] % 1024)).reshape(-1, 128)).reshape(-1)
        parts, at = [], 0
        for size in sizes:
            parts.append(flat[at : at + size])
            at += size
        parts[1] = parts[1].reshape(CONV, CC)
        collected.append((owned_out, *parts))
    owned_ins.append(late_sum(*waiting))
    collected = [(owned_in, *entry) for owned_in, entry in zip(owned_ins, collected)][::-1]
    stacked = [jnp.stack([entry[member] for entry in collected], 0) for member in range(9)]
    return (stream, grad_stream, *stacked)


def solution(mesh):
    tokens = P(("fsdp", "ctx"), None)
    sharded = P(None, "fsdp", None)
    owned = P(None, ("fsdp", "ctx"), None)
    return jax.shard_map(
        local,
        mesh=mesh,
        in_specs=(tokens, sharded, sharded) + (P(),) * 7 + (tokens,),
        out_specs=(tokens, tokens, owned, owned) + (P(),) * 7,
        check_vma=False,
    )
```

```python
import functools

import jax
import jax.numpy as jnp
from jax import lax
from jax.experimental import pallas as pl
from jax.experimental.pallas import tpu as pltpu
from jax.sharding import PartitionSpec as P

H = 48
P_SIZE = 64
N = 128
CONV = 4
LAYERS = 2
DI = 3072
CC = 3328
W = 256
G = DI // W
K = W // P_SIZE

EPS = 1e-05
HIGH = lax.Precision.HIGHEST
F32 = jnp.float32
BF = jnp.bfloat16


def mm(a, b):
    return lax.dot_general(a.astype(BF), b.astype(BF), (((1,), (0,)), ((), ())), preferred_element_type=F32)


def mm_nt(a, b):
    return lax.dot_general(a.astype(BF), b.astype(BF), (((1,), (1,)), ((), ())), preferred_element_type=F32)


def mm_tn(a, b):
    return lax.dot_general(a.astype(BF), b.astype(BF), (((0,), (0,)), ((), ())), preferred_element_type=F32)


def extend(halo_ref, conv_ref):
    return jnp.concatenate([halo_ref[...], conv_ref[...].astype(F32)], 0)


def conv_pre(ext, taps_ref, bias_ref, rows):
    acc = bias_ref[...] + ext[5 : 5 + rows] * taps_ref[0:1, :]
    for j in range(1, CONV):
        acc = acc + ext[5 + j : 5 + j + rows] * taps_ref[j : j + 1, :]
    return acc


def sigmoid(v):
    return 1.0 / (1.0 + jnp.exp(-v))


def pair_cols(col, first, low):
    return jnp.where(low, col[:, first : first + 1], col[:, first + 1 : first + 2])


def masked_scores(c_rows, b_rows):
    s = mm_nt(c_rows, b_rows)
    r = lax.broadcasted_iota(jnp.int32, s.shape, 0)
    q = lax.broadcasted_iota(jnp.int32, s.shape, 1)
    return jnp.where(r >= q, s, 0.0)


def scan_fwd_kernel(conv_ref, conv_bc_ref, halo_ref, halo_bc_ref, taps_ref, taps_bc_ref, bias_ref, bias_bc_ref,
                    col_ref, row_ref, skip_ref, y_ref, state_ref, bc_ref, s_ref):
    rows = conv_ref.shape[0]

    @pl.when(pl.program_id(0) == 0)
    def _():
        pre = conv_pre(extend(halo_bc_ref, conv_bc_ref), taps_bc_ref, bias_bc_ref, rows)
        bc = pre * sigmoid(pre)
        bc_ref[...] = bc
        s_ref[...] = masked_scores(bc[:, N:], bc[:, :N])

    pre = conv_pre(extend(halo_ref, conv_ref), taps_ref, bias_ref, rows)
    x = pre * sigmoid(pre)
    low = lax.broadcasted_iota(jnp.int32, (rows, 2 * P_SIZE), 1) < P_SIZE
    col = col_ref[0]
    row = row_ref[0]
    b_bf = bc_ref[:, :N].astype(BF)
    for pair in range(K // 2):
        h0 = 2 * pair
        cols = slice(pair * 128, pair * 128 + 128)
        x2 = x[:, cols]
        xs = x2 * pair_cols(col, K + h0, low)
        mixes, parts = [], []
        for i in range(2):
            h = h0 + i
            decay = jnp.exp(jnp.minimum(col[:, h : h + 1] - row[h : h + 1, :], 0.0))
            mixes.append((s_ref[...] * decay).astype(BF))
            parts.append(jnp.where(low if i == 0 else ~low, xs, 0.0).astype(BF))
        y = mm(jnp.concatenate(mixes, 1), jnp.concatenate(parts, 0))
        y_ref[:, cols] = y + skip_ref[:, cols] * x2
        last = jnp.where(low[:1], row[h0 : h0 + 1, rows - 1 : rows], row[h0 + 1 : h0 + 2, rows - 1 : rows])
        tail = jnp.exp(last - pair_cols(col, h0, low))
        state_ref[cols, :] = mm_tn(xs * tail, b_bf)


def gate_fwd_kernel(y_ref, gate_ref, in_ref, bc_ref, col_ref, gain_ref, ssm_ref, gn_ref, gated_ref, acc_ref):
    g = pl.program_id(0)
    rows = y_ref.shape[0]

    @pl.when(g == 0)
    def _():
        acc_ref[...] = jnp.zeros_like(acc_ref)

    low = lax.broadcasted_iota(jnp.int32, (rows, 2 * P_SIZE), 1) < P_SIZE
    col = col_ref[0]
    z = mm_nt(bc_ref[:, N:], in_ref[...])
    e = jnp.concatenate([jnp.exp(pair_cols(col, 2 * p, low)) for p in range(K // 2)], 1)
    ssm = y_ref[...] + e * z
    ssm_ref[...] = ssm
    gate = gate_ref[...]
    gated = ssm * (gate * sigmoid(gate))
    gated_ref[g] = gated
    acc_ref[...] += gated * gated

    @pl.when(g == G - 1)
    def _():
        r = lax.rsqrt(jnp.sum(acc_ref[...], 1, keepdims=True) / DI + EPS)
        for i in range(G):
            cols = slice(i * W, i * W + W)
            gn_ref[:, cols] = (gated_ref[i] * r * gain_ref[:, cols]).astype(BF)


def gate_bwd_kernel(ssm_ref, gate_ref, dn_ref, gain_ref, col_ref, bc_ref, dssm_ref, dgate_ref, ggain_ref, lg_ref,
                    sq_ref, dot_ref, r_ref, k_ref):
    phase = pl.program_id(0)
    g = pl.program_id(1)
    rows = ssm_ref.shape[0]
    ssm = ssm_ref[...]
    gate = gate_ref[...]
    sig = sigmoid(gate)
    act = gate * sig
    gated = ssm * act
    dn = dn_ref[...]
    dng = dn * gain_ref[...]

    @pl.when((phase == 0) & (g == 0))
    def _():
        sq_ref[...] = jnp.zeros_like(sq_ref)
        dot_ref[...] = jnp.zeros_like(dot_ref)

    @pl.when(phase == 0)
    def _():
        sq_ref[...] += gated * gated
        dot_ref[...] += dng * gated

    @pl.when((phase == 1) & (g == 0))
    def _():
        r = lax.rsqrt(jnp.sum(sq_ref[...], 1, keepdims=True) / DI + EPS)
        r_ref[...] = r
        k_ref[...] = r * r * r * jnp.sum(dot_ref[...], 1, keepdims=True) / DI

    @pl.when(phase == 1)
    def _():
        r = r_ref[...]
        dgated = r * dng - gated * k_ref[...]
        dssm = dgated * act
        dssm_ref[...] = dssm
        dgate_ref[...] = (dgated * ssm * (sig * (1.0 + gate * (1.0 - sig)))).astype(BF)
        ggain_ref[...] = jnp.sum(dn * (gated * r), 0, keepdims=True)
        low = lax.broadcasted_iota(jnp.int32, (rows, 2 * P_SIZE), 1) < P_SIZE
        col = col_ref[0]
        e = jnp.concatenate([jnp.exp(pair_cols(col, 2 * p, low)) for p in range(K // 2)], 1)
        lg_ref[...] = mm_tn(dssm * e, bc_ref[:, N:])


def conv_back(d_act, pre, sig, ext, taps_ref, rows):
    d_pre = d_act * (sig * (1.0 + pre * (1.0 - sig)))
    zero = jnp.zeros((8, d_pre.shape[1]), F32)
    below = jnp.concatenate([d_pre, zero], 0)
    above = jnp.concatenate([zero, d_pre[:8]], 0)
    d_conv = below[3 : 3 + rows] * taps_ref[0:1, :]
    edge = above[8:16] * taps_ref[0:1, :]
    terms = [jnp.sum(d_pre * ext[5 : 5 + rows], 0, keepdims=True)]
    for j in range(1, CONV):
        d_conv = d_conv + below[3 - j : 3 - j + rows] * taps_ref[j : j + 1, :]
        edge = edge + above[8 - j : 16 - j] * taps_ref[j : j + 1, :]
        terms.append(jnp.sum(d_pre * ext[5 + j : 5 + j + rows], 0, keepdims=True))
    terms.append(jnp.sum(d_pre, 0, keepdims=True))
    return d_conv, edge, terms


def scan_bwd_kernel(conv_ref, conv_bc_ref, halo_ref, halo_bc_ref, taps_ref, taps_bc_ref, bias_ref, bias_bc_ref,
                    col_ref, row_ref, skip_ref, bc_ref, dy_ref, in_ref, out_ref,
                    dconv_ref, edge_ref, gt_ref, dconv_bc_ref, edge_bc_ref, gt_bc_ref, colo_ref, rowo_ref, misc_ref,
                    s_ref, ds_ref, dbc_ref):
    g = pl.program_id(0)
    rows = conv_ref.shape[0]

    @pl.when(g == 0)
    def _():
        s_ref[...] = masked_scores(bc_ref[:, N:], bc_ref[:, :N])
        ds_ref[...] = jnp.zeros_like(ds_ref)
        dbc_ref[...] = jnp.zeros_like(dbc_ref)

    ext = extend(halo_ref, conv_ref)
    pre = conv_pre(ext, taps_ref, bias_ref, rows)
    sig = sigmoid(pre)
    x = pre * sig
    low = lax.broadcasted_iota(jnp.int32, (rows, 2 * P_SIZE), 1) < P_SIZE
    lane = lax.broadcasted_iota(jnp.int32, (rows, 2 * K), 1)
    col = col_ref[0]
    row = row_ref[0]
    b_bf = bc_ref[:, :N].astype(BF)
    c_bf = bc_ref[:, N:].astype(BF)
    colo = jnp.zeros((rows, 2 * K), F32)
    dxs = []
    misc_ref[...] = jnp.zeros_like(misc_ref)
    rowo_ref[...] = jnp.zeros_like(rowo_ref)
    for pair in range(K // 2):
        h0 = 2 * pair
        cols = slice(pair * 128, pair * 128 + 128)
        x2 = x[:, cols]
        step = pair_cols(col, K + h0, low)
        xs = x2 * step
        xs_bf = xs.astype(BF)
        dy = dy_ref[:, cols]
        h_in = in_ref[cols, :]
        h_out = out_ref[cols, :]
        cum = pair_cols(col, h0, low)
        e = jnp.exp(cum)
        last = jnp.where(low[:1], row[h0 : h0 + 1, rows - 1 : rows], row[h0 + 1 : h0 + 2, rows - 1 : rows])
        tail = jnp.exp(last - cum)
        edy = e * dy
        txs = tail * xs
        inter = edy * mm_nt(c_bf, h_in)
        u = mm_nt(b_bf, h_out)
        r = txs * u
        dbc_ref[:, N:] += mm(edy, h_in)
        dbc_ref[:, :N] += mm(txs, h_out)
        d_xs = tail * u
        side = inter - r
        for i in range(2):
            h = h0 + i
            keep = low if i == 0 else ~low
            dyh = jnp.where(keep, dy, 0.0).astype(BF)
            d_mix = mm_nt(dyh, xs_bf)
            decay = jnp.exp(jnp.minimum(col[:, h : h + 1] - row[h : h + 1, :], 0.0))
            d_ld = d_mix * decay
            ds_ref[...] += d_ld
            s = s_ref[...]
            weight = d_ld * s
            d_xs = d_xs + mm_tn(s * decay, dyh)
            rowo_ref[0, h : h + 1, :] = jnp.sum(weight, 0, keepdims=True)
            folded = weight[:, :128] + weight[:, 128:] + jnp.where(keep, side, 0.0)
            colo = jnp.where(lane == h, jnp.sum(folded, 1, keepdims=True), colo)
        prod = x2 * d_xs
        for i in range(2):
            keep = low if i == 0 else ~low
            s_sum = jnp.sum(jnp.where(keep, prod, 0.0), 1, keepdims=True)
            colo = jnp.where(lane == K + h0 + i, s_sum, colo)
        dxs.append(step * d_xs + skip_ref[:, cols] * dy)
        hg = h_in.astype(F32) * h_out.astype(F32)
        misc_ref[0, 0:1, cols] = jnp.sum(dy * x2, 0, keepdims=True)
        misc_ref[0, 1:2, cols] = jnp.sum(r, 0, keepdims=True)
        misc_ref[0, 2:3, cols] = jnp.sum(hg[:P_SIZE], 0, keepdims=True)
        misc_ref[0, 3:4, cols] = jnp.sum(hg[P_SIZE:], 0, keepdims=True)
    colo_ref[0] = colo
    d_conv, edge, terms = conv_back(jnp.concatenate(dxs, 1), pre, sig, ext, taps_ref, rows)
    dconv_ref[...] = d_conv
    edge_ref[...] = edge
    gt_ref[...] = jnp.zeros_like(gt_ref)
    for j, term in enumerate(terms):
        gt_ref[j : j + 1, :] = term

    @pl.when(g == G - 1)
    def _():
        r_i = lax.broadcasted_iota(jnp.int32, ds_ref.shape, 0)
        q_i = lax.broadcasted_iota(jnp.int32, ds_ref.shape, 1)
        ds = jnp.where(r_i >= q_i, ds_ref[...], 0.0).astype(BF)
        d_c = dbc_ref[:, N:] + mm(ds, b_bf)
        d_b = dbc_ref[:, :N] + mm_tn(ds, c_bf)
        ext2 = extend(halo_bc_ref, conv_bc_ref)
        pre2 = conv_pre(ext2, taps_bc_ref, bias_bc_ref, rows)
        d_conv2, edge2, terms2 = conv_back(
            jnp.concatenate([d_b, d_c], 1), pre2, sigmoid(pre2), ext2, taps_bc_ref, rows)
        dconv_bc_ref[...] = d_conv2
        edge_bc_ref[...] = edge2
        gt_bc_ref[...] = jnp.zeros_like(gt_bc_ref)
        for j, term in enumerate(terms2):
            gt_bc_ref[j : j + 1, :] = term


def col_block(rows):
    return pl.BlockSpec((rows, W), lambda g: (0, g))


def bc_block(rows):
    return pl.BlockSpec((rows, W), lambda g: (0, G))


def fixed(shape):
    return pl.BlockSpec(shape, lambda g: (0,) * len(shape))


def packs(rows):
    return [pl.BlockSpec((1, rows, 2 * K), lambda g: (g, 0, 0)), pl.BlockSpec((1, 2 * K, rows), lambda g: (g, 0, 0))]


def conv_specs(rows):
    return [col_block(rows), bc_block(rows), col_block(8), bc_block(8), col_block(CONV), bc_block(CONV),
            col_block(1), bc_block(1)] + packs(rows) + [col_block(1)]


STATE = pl.BlockSpec((W, N), lambda g: (g, 0))


def sds(shape, dtype=F32):
    return jax.ShapeDtypeStruct(shape, dtype)


def scan_fwd(conv_in, halo, taps, bias, col, row, skip):
    rows = conv_in.shape[0]
    return pl.pallas_call(
        scan_fwd_kernel,
        grid=(G,),
        in_specs=conv_specs(rows),
        out_specs=[col_block(rows), STATE, fixed((rows, 2 * N))],
        out_shape=[sds((rows, DI)), sds((DI, N)), sds((rows, 2 * N))],
        scratch_shapes=[pltpu.VMEM((rows, rows), F32)],
        name="scan_fwd",
    )(conv_in, conv_in, halo, halo, taps, taps, bias, bias, col, row, skip)


def gate_fwd(y, gate, incoming, bc, col, gain):
    rows = y.shape[0]
    return pl.pallas_call(
        gate_fwd_kernel,
        grid=(G,),
        in_specs=[col_block(rows), col_block(rows), STATE, fixed((rows, 2 * N)), packs(rows)[0], fixed((1, DI))],
        out_specs=[col_block(rows), fixed((rows, DI))],
        out_shape=[sds((rows, DI)), sds((rows, DI), BF)],
        scratch_shapes=[pltpu.VMEM((G, rows, W), F32), pltpu.VMEM((rows, W), F32)],
        name="gate_fwd",
    )(y, gate, incoming, bc, col, gain)


def gate_bwd(ssm, gate, dn, gain, col, bc):
    rows = ssm.shape[0]
    block = pl.BlockSpec((rows, W), lambda p, g: (0, g))
    late = pl.BlockSpec((rows, W), lambda p, g: (0, p * g))
    return pl.pallas_call(
        gate_bwd_kernel,
        grid=(2, G),
        in_specs=[block, block, block, pl.BlockSpec((1, W), lambda p, g: (0, g)),
                  pl.BlockSpec((1, rows, 2 * K), lambda p, g: (g, 0, 0)),
                  pl.BlockSpec((rows, 2 * N), lambda p, g: (0, 0))],
        out_specs=[late, late, pl.BlockSpec((1, W), lambda p, g: (0, p * g)),
                   pl.BlockSpec((W, N), lambda p, g: (p * g, 0))],
        out_shape=[sds((rows, DI)), sds((rows, DI), BF), sds((1, DI)), sds((DI, N))],
        scratch_shapes=[pltpu.VMEM((rows, W), F32), pltpu.VMEM((rows, W), F32),
                        pltpu.VMEM((rows, 1), F32), pltpu.VMEM((rows, 1), F32)],
        name="gate_bwd",
    )(ssm, gate, dn, gain, col, bc)


def scan_bwd(conv_in, halo, taps, bias, col, row, skip, bc, dy, incoming, outgoing):
    rows = conv_in.shape[0]
    return pl.pallas_call(
        scan_bwd_kernel,
        grid=(G,),
        in_specs=conv_specs(rows) + [fixed((rows, 2 * N)), col_block(rows), STATE, STATE],
        out_specs=[col_block(rows), col_block(8), col_block(8), fixed((rows, W)), fixed((8, W)), fixed((8, W))]
        + packs(rows) + [pl.BlockSpec((1, 8, W), lambda g: (g, 0, 0))],
        out_shape=[sds((rows, DI)), sds((8, DI)), sds((8, DI)), sds((rows, W)), sds((8, W)), sds((8, W)),
                   sds((G, rows, 2 * K)), sds((G, 2 * K, rows)), sds((G, 8, W))],
        scratch_shapes=[pltpu.VMEM((rows, rows), F32), pltpu.VMEM((rows, rows), F32), pltpu.VMEM((rows, 2 * N), F32)],
        name="scan_bwd",
    )(conv_in, conv_in, halo, halo, taps, taps, bias, bias, col, row, skip, bc, dy, incoming, outgoing)


def passed_along(value, axis, steps):
    count = lax.axis_size(axis)
    initial, last = (max(0, -steps), min(count, count - steps))
    return lax.ppermute(value, axis, [(source, source + steps) for source in range(initial, last)])


CHUNKS = 2


def carry(totals, local_state, steps):
    hops = lax.axis_size("ctx") - 1
    size = DI // CHUNKS
    parts = []
    for chunk in range(CHUNKS):
        rows = slice(chunk * size, chunk * size + size)
        own, factor = local_state[rows], totals[rows]
        incoming = passed_along(own.astype(BF), "ctx", steps)
        for _ in range(hops - 1):
            incoming = passed_along((factor * incoming.astype(F32) + own).astype(BF), "ctx", steps)
        parts.append(incoming)
    return jnp.concatenate(parts, 0)


def all_sum(value):
    for axis in ("fsdp", "ctx"):
        count = lax.axis_size(axis)
        if count & (count - 1):
            value = lax.psum(value, axis)
            continue
        bit = 1
        while bit < count:
            value = value + lax.ppermute(value, axis, [(i, i ^ bit) for i in range(count)])
            bit *= 2
    return value


def rms_norm(values, gain_row):
    return values * lax.rsqrt(jnp.mean(values * values, axis=-1, keepdims=True) + EPS) * gain_row


def rows_product(left, right):
    return lax.dot_general(left, right, (((0,), (0,)), ((), ())), preferred_element_type=F32)


def right_transposed(left, right):
    return lax.dot_general(left, right, (((1,), (1,)), ((), ())), preferred_element_type=F32)


def gathered(value):
    return lax.all_gather(value, "fsdp", axis=0, tiled=True)


def to_owners(split):
    moved = lax.all_to_all(jnp.transpose(split, (1, 0, 2)), "fsdp", split_axis=0, concat_axis=0, tiled=True)
    return moved.reshape(-1, split.shape[2])


def by_run(part):
    fsdp_count, ctx_count = lax.axis_size("fsdp"), lax.axis_size("ctx")
    rows, width = part.shape
    own = rows // (fsdp_count * ctx_count)
    blocks = part.astype(BF).reshape(fsdp_count, ctx_count, own, width)
    return jnp.transpose(blocks, (1, 0, 2, 3)).reshape(ctx_count, fsdp_count * own, width)


def run_sum(blocks):
    flat = blocks.reshape(-1, blocks.shape[2])
    return lax.psum_scatter(flat, "ctx", scatter_dimension=0, tiled=True)


def gate_parts(normed_all, d_gate):
    fsdp_count = lax.axis_size("fsdp")
    return by_run(rows_product(normed_all, to_owners(d_gate.reshape(d_gate.shape[0], fsdp_count, -1))))


def out_parts(norm_cols, grad_all):
    ctx_count = lax.axis_size("ctx")
    width, model = norm_cols.shape[1], grad_all.shape[1]
    part = rows_product(norm_cols, grad_all).astype(BF)
    part = part.reshape(ctx_count, width // ctx_count, model // width, width)
    return jnp.transpose(part, (0, 2, 1, 3)).reshape(ctx_count, -1, width)


def early_sum(part_gate, part_out, model):
    summed = run_sum(jnp.concatenate([part_gate, part_out], 1))
    in_rows, width = part_gate.shape[1:]
    owned_out = jnp.transpose(summed[in_rows:].reshape(model // width, -1, width), (1, 0, 2))
    return summed[:in_rows], owned_out.reshape(-1, model).astype(F32)


def rest_owners(d_rest):
    fsdp_count = lax.axis_size("fsdp")
    rows = d_rest.shape[0]
    wide = d_rest[:, :DI].reshape(rows, fsdp_count, -1)
    narrow = d_rest[:, DI:].reshape(rows, fsdp_count, -1)
    width = wide.shape[2] + narrow.shape[2]
    return to_owners(jnp.concatenate([wide, narrow, jnp.zeros((rows, fsdp_count, -width % 128), BF)], 2))


def rest_parts(normed_all, rest_cols):
    width = (CC - DI + H + DI) // lax.axis_size("fsdp")
    return by_run(rows_product(normed_all, rest_cols)[:, :width])


def late_sum(part_rest, gate_sum):
    fsdp_count = lax.axis_size("fsdp")
    width = gate_sum.shape[1]
    both = jnp.concatenate([gate_sum, run_sum(part_rest)], 1)
    both = both.reshape(fsdp_count, -1, both.shape[1])
    both = lax.all_to_all(both, "fsdp", split_axis=0, concat_axis=0, tiled=True)
    both = jnp.transpose(both, (1, 0, 2))
    own = both.shape[0]
    parts = (both[:, :, :width], both[:, :, width : 2 * width], both[:, :, 2 * width :])
    return jnp.concatenate([part.reshape(own, -1) for part in parts], 1).astype(F32)


def grouped(cum, steps):
    rows = cum.shape[0]
    both = jnp.stack([cum.reshape(rows, G, K), steps.reshape(rows, G, K)], 2).reshape(rows, G, 2 * K)
    return jnp.transpose(both, (1, 0, 2)), jnp.transpose(both, (1, 2, 0))


def local(
    activations,
    in_weight,
    out_weight,
    norm_gain,
    conv_weight,
    conv_bias,
    step_bias,
    decay_log,
    skip_gain,
    gate_gain,
    cotangent,
):
    rows = activations.shape[0]
    edge_count = CONV - 1
    order = jnp.arange(rows)
    lower = (order[:, None] >= order[None, :]).astype(F32)
    model = out_weight.shape[2]
    first = gathered(in_weight[0])
    weights = [(first[:, DI:], first[:, :DI], gathered(out_weight[0]))]
    for k in range(1, LAYERS):
        weights.append((gathered(in_weight[k][:, DI:]), gathered(in_weight[k][:, :DI]), gathered(out_weight[k])))
    stream = activations
    kept = []
    for k in range(LAYERS):
        w_conv, w_gate, w_out = weights[k]
        normed = rms_norm(stream, norm_gain[k]).astype(BF)
        proj = jnp.dot(normed, w_conv, preferred_element_type=F32)
        conv_in = proj[:, :CC].astype(BF)
        raw_steps = proj[:, CC:]
        edge_in = passed_along(conv_in[rows - edge_count :], "ctx", 1)
        halo = jnp.concatenate([jnp.zeros((8 - edge_count, CC), F32), edge_in.astype(F32)], 0)
        steps = jax.nn.softplus(raw_steps + step_bias[k][None, :])
        cum = jnp.dot(lower, -steps * jnp.exp(decay_log[k])[None, :], precision=HIGH)
        col, row = grouped(cum, steps)
        totals = jnp.repeat(jnp.exp(cum[-1]), P_SIZE)[:, None]
        skip = jnp.repeat(skip_gain[k], P_SIZE)[None, :]
        bias = conv_bias[k][None, :]
        y, state, bc = scan_fwd(conv_in, halo, conv_weight[k], bias, col, row, skip)
        gate_in = jnp.dot(normed, w_gate, preferred_element_type=F32)
        incoming = carry(totals, state, 1)
        ssm, gnormed = gate_fwd(y, gate_in, incoming, bc, col, gate_gain[k][None, :])
        kept.append((stream, normed, gate_in, conv_in, halo, raw_steps, steps, col, row, totals, skip, bias, bc,
                     incoming, ssm, gnormed))
        stream = stream + jnp.dot(gnormed, w_out, preferred_element_type=F32)
    grad_stream = cotangent
    gnormed_cols = to_owners(kept[-1][-1].reshape(rows, lax.axis_size("fsdp"), -1))
    collected, owned_ins, waiting = [], [], None
    for k in reversed(range(LAYERS)):
        w_conv, w_gate, w_out = weights[k]
        (stream_in, normed, gate_in, conv_in, halo, raw_steps, steps, col, row, totals, skip, bias, bc,
         incoming, ssm, gnormed) = kept[k]
        grad_bf = grad_stream.astype(BF)
        d_gnormed = right_transposed(grad_bf, w_out)
        d_ssm, d_gate, g_gate, local_grad = gate_bwd(ssm, gate_in, d_gnormed, gate_gain[k][None, :], col, bc)
        tokens = jnp.concatenate([normed, grad_bf], 1)
        if waiting is not None:
            local_grad, rest_cols = lax.optimization_barrier((local_grad, waiting[1]))
            tokens, gate_sum = lax.optimization_barrier((tokens, waiting[2]))
        tokens = gathered(tokens)
        outgoing = carry(totals, local_grad, -1)
        normed_all, grad_all = tokens[:, :model], tokens[:, model:]
        part_gate = gate_parts(normed_all, d_gate)
        part_out = out_parts(gnormed_cols, grad_all)
        if waiting is None:
            outgoing, part_gate, part_out = lax.optimization_barrier((outgoing, part_gate, part_out))
        else:
            part_rest = rest_parts(waiting[0], rest_cols)
            outgoing, part_gate, part_out, part_rest = lax.optimization_barrier(
                (outgoing, part_gate, part_out, part_rest))
            owned_ins.append(late_sum(part_rest, gate_sum))
        if k:
            outgoing, next_gnormed = lax.optimization_barrier((outgoing, kept[k - 1][-1]))
            gnormed_cols = to_owners(next_gnormed.reshape(rows, lax.axis_size("fsdp"), -1))
        gate_sum, owned_out = early_sum(part_gate, part_out, model)
        d_x, edge_x, gt_x, d_bc, edge_bc, gt_bc, colo, rowo, misc = scan_bwd(
            conv_in, halo, conv_weight[k], bias, col, row, skip, bc, d_ssm, incoming, outgoing)
        if k:
            d_x, gnormed_cols = lax.optimization_barrier((d_x, gnormed_cols))
        edges = jnp.concatenate([edge_x[:edge_count], edge_bc[:edge_count]], 1)
        edge_back = passed_along(edges, "ctx", -1)
        taps_grad = jnp.concatenate([gt_x, gt_bc], 1)
        colf = jnp.transpose(colo, (1, 0, 2))
        d_cum = colf[:, :, :K].reshape(rows, H) - jnp.transpose(rowo[:, :K], (2, 0, 1)).reshape(rows, H)
        g_skip = misc[:, 0].reshape(H, P_SIZE).sum(1)
        r_sum = misc[:, 1].reshape(H, P_SIZE).sum(1)
        hg = jnp.transpose(misc[:, 2:4].reshape(G, 2, 2, N), (0, 2, 1, 3)).sum(-1).reshape(H)
        d_last = r_sum + totals[::P_SIZE, 0] * hg
        d_cum = d_cum + jnp.where(order[:, None] == rows - 1, d_last[None, :], 0.0)
        d_log = jnp.dot(lower.T, d_cum, precision=HIGH)
        rate = jnp.exp(decay_log[k])[None, :]
        d_step = colf[:, :, K:].reshape(rows, H) - d_log * rate
        d_raw = d_step * jax.nn.sigmoid(raw_steps + step_bias[k][None, :])
        g_bias = d_raw.sum(0)
        g_log = -(d_log * steps * rate).sum(0)
        d_conv = jnp.concatenate([d_x, d_bc], 1)
        d_conv = d_conv + jnp.pad(edge_back, ((rows - edge_count, 0), (0, 0)))
        d_rest = jnp.concatenate([d_conv, d_raw], 1).astype(BF)
        d_normed = right_transposed(d_gate, w_gate) + right_transposed(d_rest, w_conv)
        _, pullback = jax.vjp(rms_norm, stream_in, norm_gain[k])
        d_stream, g_norm = pullback(d_normed)
        grad_stream = grad_stream + d_stream
        waiting = (normed_all, rest_owners(d_rest), gate_sum)
        small = [g_norm, taps_grad[:CONV].reshape(-1), taps_grad[CONV], g_bias, g_log, g_skip, g_gate.reshape(-1)]
        collected.append((owned_out, small))
    sizes = [part.shape[0] for part in collected[0][1]]
    flat = jnp.concatenate([part for entry in collected[::-1] for part in entry[1]])
    flat = jnp.pad(flat, (0, -flat.shape[0] % 1024)).reshape(-1, 128)
    flat, part_rest = lax.optimization_barrier((flat, rest_parts(waiting[0], waiting[1])))
    owned_ins.append(late_sum(part_rest, waiting[2]))
    flat = all_sum(flat).reshape(-1)[: LAYERS * sum(sizes)].reshape(LAYERS, -1)
    stacked = [jnp.stack(owned_ins[::-1], 0), jnp.stack([entry[0] for entry in collected[::-1]], 0)]
    at = 0
    for size in sizes:
        stacked.append(flat[:, at : at + size])
        at += size
    stacked[3] = stacked[3].reshape(LAYERS, CONV, CC)
    return (stream, grad_stream, *stacked)


def solution(mesh):
    tokens = P(("fsdp", "ctx"), None)
    sharded = P(None, "fsdp", None)
    owned = P(None, ("fsdp", "ctx"), None)
    return jax.shard_map(
        local,
        mesh=mesh,
        in_specs=(tokens, sharded, sharded) + (P(),) * 7 + (tokens,),
        out_specs=(tokens, tokens, owned, owned) + (P(),) * 7,
        check_vma=False,
    )
```

```python
import functools

import jax
import jax.numpy as jnp
from jax import lax
from jax.experimental import pallas as pl
from jax.experimental.layout import Layout, with_layout_constraint
from jax.experimental.pallas import tpu as pltpu
from jax.sharding import PartitionSpec as P

H = 48
P_SIZE = 64
N = 128
CONV = 4
LAYERS = 2
DI = 3072
CC = 3328
W = 256
G = DI // W
K = W // P_SIZE

EPS = 1e-05
HIGH = lax.Precision.HIGHEST
F32 = jnp.float32
BF = jnp.bfloat16


def mm(a, b):
    return lax.dot_general(a.astype(BF), b.astype(BF), (((1,), (0,)), ((), ())), preferred_element_type=F32)


def mm_nt(a, b):
    return lax.dot_general(a.astype(BF), b.astype(BF), (((1,), (1,)), ((), ())), preferred_element_type=F32)


def mm_tn(a, b):
    return lax.dot_general(a.astype(BF), b.astype(BF), (((0,), (0,)), ((), ())), preferred_element_type=F32)


def extend(halo_ref, conv_ref):
    return jnp.concatenate([halo_ref[...], conv_ref[...].astype(F32)], 0)


def conv_pre(ext, taps_ref, bias_ref, rows):
    acc = bias_ref[...] + ext[5 : 5 + rows] * taps_ref[0:1, :]
    for j in range(1, CONV):
        acc = acc + ext[5 + j : 5 + j + rows] * taps_ref[j : j + 1, :]
    return acc


def sigmoid(v):
    return 1.0 / (1.0 + jnp.exp(-v))


def pair_cols(col, first, low):
    return jnp.where(low, col[:, first : first + 1], col[:, first + 1 : first + 2])


def masked_scores(c_rows, b_rows):
    s = mm_nt(c_rows, b_rows)
    r = lax.broadcasted_iota(jnp.int32, s.shape, 0)
    q = lax.broadcasted_iota(jnp.int32, s.shape, 1)
    return jnp.where(r >= q, s, 0.0)


def scan_fwd_kernel(conv_ref, conv_bc_ref, halo_ref, halo_bc_ref, taps_ref, taps_bc_ref, bias_ref, bias_bc_ref,
                    col_ref, row_ref, skip_ref, y_ref, state_ref, bc_ref, s_ref):
    rows = conv_ref.shape[0]

    @pl.when(pl.program_id(0) == 0)
    def _():
        pre = conv_pre(extend(halo_bc_ref, conv_bc_ref), taps_bc_ref, bias_bc_ref, rows)
        bc = pre * sigmoid(pre)
        bc_ref[...] = bc
        s_ref[...] = masked_scores(bc[:, N:], bc[:, :N])

    pre = conv_pre(extend(halo_ref, conv_ref), taps_ref, bias_ref, rows)
    x = pre * sigmoid(pre)
    low = lax.broadcasted_iota(jnp.int32, (rows, 2 * P_SIZE), 1) < P_SIZE
    col = col_ref[0]
    row = row_ref[0]
    b_bf = bc_ref[:, :N].astype(BF)
    for pair in range(K // 2):
        h0 = 2 * pair
        cols = slice(pair * 128, pair * 128 + 128)
        x2 = x[:, cols]
        xs = x2 * pair_cols(col, K + h0, low)
        mixes, parts = [], []
        for i in range(2):
            h = h0 + i
            decay = jnp.exp(jnp.minimum(col[:, h : h + 1] - row[h : h + 1, :], 0.0))
            mixes.append((s_ref[...] * decay).astype(BF))
            parts.append(jnp.where(low if i == 0 else ~low, xs, 0.0).astype(BF))
        y = mm(jnp.concatenate(mixes, 1), jnp.concatenate(parts, 0))
        y_ref[:, cols] = y + skip_ref[:, cols] * x2
        last = jnp.where(low[:1], row[h0 : h0 + 1, rows - 1 : rows], row[h0 + 1 : h0 + 2, rows - 1 : rows])
        tail = jnp.exp(last - pair_cols(col, h0, low))
        state_ref[cols, :] = mm_tn(xs * tail, b_bf)


def gate_fwd_kernel(y_ref, gate_ref, in_ref, bc_ref, col_ref, gain_ref, ssm_ref, gn_ref, gated_ref, acc_ref):
    g = pl.program_id(0)
    rows = y_ref.shape[0]

    @pl.when(g == 0)
    def _():
        acc_ref[...] = jnp.zeros_like(acc_ref)

    low = lax.broadcasted_iota(jnp.int32, (rows, 2 * P_SIZE), 1) < P_SIZE
    col = col_ref[0]
    z = mm_nt(bc_ref[:, N:], in_ref[...])
    e = jnp.concatenate([jnp.exp(pair_cols(col, 2 * p, low)) for p in range(K // 2)], 1)
    ssm = y_ref[...] + e * z
    ssm_ref[...] = ssm
    gate = gate_ref[...]
    gated = ssm * (gate * sigmoid(gate))
    gated_ref[g] = gated
    acc_ref[...] += gated * gated

    @pl.when(g == G - 1)
    def _():
        r = lax.rsqrt(jnp.sum(acc_ref[...], 1, keepdims=True) / DI + EPS)
        for i in range(G):
            cols = slice(i * W, i * W + W)
            gn_ref[:, cols] = (gated_ref[i] * r * gain_ref[:, cols]).astype(BF)


def gate_bwd_kernel(ssm_ref, gate_ref, dn_ref, gain_ref, col_ref, bc_ref, dssm_ref, dgate_ref, ggain_ref, lg_ref,
                    sq_ref, dot_ref, r_ref, k_ref):
    phase = pl.program_id(0)
    g = pl.program_id(1)
    rows = ssm_ref.shape[0]
    ssm = ssm_ref[...]
    gate = gate_ref[...]
    sig = sigmoid(gate)
    act = gate * sig
    gated = ssm * act
    dn = dn_ref[...]
    dng = dn * gain_ref[...]

    @pl.when((phase == 0) & (g == 0))
    def _():
        sq_ref[...] = jnp.zeros_like(sq_ref)
        dot_ref[...] = jnp.zeros_like(dot_ref)

    @pl.when(phase == 0)
    def _():
        sq_ref[...] += gated * gated
        dot_ref[...] += dng * gated

    @pl.when((phase == 1) & (g == 0))
    def _():
        r = lax.rsqrt(jnp.sum(sq_ref[...], 1, keepdims=True) / DI + EPS)
        r_ref[...] = r
        k_ref[...] = r * r * r * jnp.sum(dot_ref[...], 1, keepdims=True) / DI

    @pl.when(phase == 1)
    def _():
        r = r_ref[...]
        dgated = r * dng - gated * k_ref[...]
        dssm = dgated * act
        dssm_ref[...] = dssm
        dgate_ref[...] = (dgated * ssm * (sig * (1.0 + gate * (1.0 - sig)))).astype(BF)
        ggain_ref[...] = jnp.sum(dn * (gated * r), 0, keepdims=True)
        low = lax.broadcasted_iota(jnp.int32, (rows, 2 * P_SIZE), 1) < P_SIZE
        col = col_ref[0]
        e = jnp.concatenate([jnp.exp(pair_cols(col, 2 * p, low)) for p in range(K // 2)], 1)
        lg_ref[...] = mm_tn(dssm * e, bc_ref[:, N:])


def conv_back(d_act, pre, sig, ext, taps_ref, rows):
    d_pre = d_act * (sig * (1.0 + pre * (1.0 - sig)))
    zero = jnp.zeros((8, d_pre.shape[1]), F32)
    below = jnp.concatenate([d_pre, zero], 0)
    above = jnp.concatenate([zero, d_pre[:8]], 0)
    d_conv = below[3 : 3 + rows] * taps_ref[0:1, :]
    edge = above[8:16] * taps_ref[0:1, :]
    terms = [jnp.sum(d_pre * ext[5 : 5 + rows], 0, keepdims=True)]
    for j in range(1, CONV):
        d_conv = d_conv + below[3 - j : 3 - j + rows] * taps_ref[j : j + 1, :]
        edge = edge + above[8 - j : 16 - j] * taps_ref[j : j + 1, :]
        terms.append(jnp.sum(d_pre * ext[5 + j : 5 + j + rows], 0, keepdims=True))
    terms.append(jnp.sum(d_pre, 0, keepdims=True))
    return d_conv, edge, terms


def scan_bwd_kernel(conv_ref, conv_bc_ref, halo_ref, halo_bc_ref, taps_ref, taps_bc_ref, bias_ref, bias_bc_ref,
                    col_ref, row_ref, skip_ref, bc_ref, dy_ref, in_ref, out_ref,
                    dconv_ref, edge_ref, gt_ref, dconv_bc_ref, edge_bc_ref, gt_bc_ref, colo_ref, rowo_ref, misc_ref,
                    s_ref, ds_ref, dbc_ref):
    g = pl.program_id(0)
    rows = conv_ref.shape[0]

    @pl.when(g == 0)
    def _():
        s_ref[...] = masked_scores(bc_ref[:, N:], bc_ref[:, :N])
        ds_ref[...] = jnp.zeros_like(ds_ref)
        dbc_ref[...] = jnp.zeros_like(dbc_ref)

    ext = extend(halo_ref, conv_ref)
    pre = conv_pre(ext, taps_ref, bias_ref, rows)
    sig = sigmoid(pre)
    x = pre * sig
    low = lax.broadcasted_iota(jnp.int32, (rows, 2 * P_SIZE), 1) < P_SIZE
    lane = lax.broadcasted_iota(jnp.int32, (rows, 2 * K), 1)
    col = col_ref[0]
    row = row_ref[0]
    b_bf = bc_ref[:, :N].astype(BF)
    c_bf = bc_ref[:, N:].astype(BF)
    colo = jnp.zeros((rows, 2 * K), F32)
    dxs = []
    misc_ref[...] = jnp.zeros_like(misc_ref)
    rowo_ref[...] = jnp.zeros_like(rowo_ref)
    for pair in range(K // 2):
        h0 = 2 * pair
        cols = slice(pair * 128, pair * 128 + 128)
        x2 = x[:, cols]
        step = pair_cols(col, K + h0, low)
        xs = x2 * step
        xs_bf = xs.astype(BF)
        dy = dy_ref[:, cols]
        h_in = in_ref[cols, :]
        h_out = out_ref[cols, :]
        cum = pair_cols(col, h0, low)
        e = jnp.exp(cum)
        last = jnp.where(low[:1], row[h0 : h0 + 1, rows - 1 : rows], row[h0 + 1 : h0 + 2, rows - 1 : rows])
        tail = jnp.exp(last - cum)
        edy = e * dy
        txs = tail * xs
        inter = edy * mm_nt(c_bf, h_in)
        u = mm_nt(b_bf, h_out)
        r = txs * u
        dbc_ref[:, N:] += mm(edy, h_in)
        dbc_ref[:, :N] += mm(txs, h_out)
        d_xs = tail * u
        side = inter - r
        for i in range(2):
            h = h0 + i
            keep = low if i == 0 else ~low
            dyh = jnp.where(keep, dy, 0.0).astype(BF)
            d_mix = mm_nt(dyh, xs_bf)
            decay = jnp.exp(jnp.minimum(col[:, h : h + 1] - row[h : h + 1, :], 0.0))
            d_ld = d_mix * decay
            ds_ref[...] += d_ld
            s = s_ref[...]
            weight = d_ld * s
            d_xs = d_xs + mm_tn(s * decay, dyh)
            rowo_ref[0, h : h + 1, :] = jnp.sum(weight, 0, keepdims=True)
            folded = weight[:, :128] + weight[:, 128:] + jnp.where(keep, side, 0.0)
            colo = jnp.where(lane == h, jnp.sum(folded, 1, keepdims=True), colo)
        prod = x2 * d_xs
        for i in range(2):
            keep = low if i == 0 else ~low
            s_sum = jnp.sum(jnp.where(keep, prod, 0.0), 1, keepdims=True)
            colo = jnp.where(lane == K + h0 + i, s_sum, colo)
        dxs.append(step * d_xs + skip_ref[:, cols] * dy)
        hg = h_in.astype(F32) * h_out.astype(F32)
        misc_ref[0, 0:1, cols] = jnp.sum(dy * x2, 0, keepdims=True)
        misc_ref[0, 1:2, cols] = jnp.sum(r, 0, keepdims=True)
        misc_ref[0, 2:3, cols] = jnp.sum(hg[:P_SIZE], 0, keepdims=True)
        misc_ref[0, 3:4, cols] = jnp.sum(hg[P_SIZE:], 0, keepdims=True)
    colo_ref[0] = colo
    d_conv, edge, terms = conv_back(jnp.concatenate(dxs, 1), pre, sig, ext, taps_ref, rows)
    dconv_ref[...] = d_conv
    edge_ref[...] = edge
    gt_ref[...] = jnp.zeros_like(gt_ref)
    for j, term in enumerate(terms):
        gt_ref[j : j + 1, :] = term

    @pl.when(g == G - 1)
    def _():
        r_i = lax.broadcasted_iota(jnp.int32, ds_ref.shape, 0)
        q_i = lax.broadcasted_iota(jnp.int32, ds_ref.shape, 1)
        ds = jnp.where(r_i >= q_i, ds_ref[...], 0.0).astype(BF)
        d_c = dbc_ref[:, N:] + mm(ds, b_bf)
        d_b = dbc_ref[:, :N] + mm_tn(ds, c_bf)
        ext2 = extend(halo_bc_ref, conv_bc_ref)
        pre2 = conv_pre(ext2, taps_bc_ref, bias_bc_ref, rows)
        d_conv2, edge2, terms2 = conv_back(
            jnp.concatenate([d_b, d_c], 1), pre2, sigmoid(pre2), ext2, taps_bc_ref, rows)
        dconv_bc_ref[...] = d_conv2
        edge_bc_ref[...] = edge2
        gt_bc_ref[...] = jnp.zeros_like(gt_bc_ref)
        for j, term in enumerate(terms2):
            gt_bc_ref[j : j + 1, :] = term


def col_block(rows):
    return pl.BlockSpec((rows, W), lambda g: (0, g))


def bc_block(rows):
    return pl.BlockSpec((rows, W), lambda g: (0, G))


def fixed(shape):
    return pl.BlockSpec(shape, lambda g: (0,) * len(shape))


def packs(rows):
    return [pl.BlockSpec((1, rows, 2 * K), lambda g: (g, 0, 0)), pl.BlockSpec((1, 2 * K, rows), lambda g: (g, 0, 0))]


def conv_specs(rows):
    return [col_block(rows), bc_block(rows), col_block(8), bc_block(8), col_block(CONV), bc_block(CONV),
            col_block(1), bc_block(1)] + packs(rows) + [col_block(1)]


STATE = pl.BlockSpec((W, N), lambda g: (g, 0))


def sds(shape, dtype=F32):
    return jax.ShapeDtypeStruct(shape, dtype)


def scan_fwd(conv_in, halo, taps, bias, col, row, skip):
    rows = conv_in.shape[0]
    return pl.pallas_call(
        scan_fwd_kernel,
        grid=(G,),
        in_specs=conv_specs(rows),
        out_specs=[col_block(rows), STATE, fixed((rows, 2 * N))],
        out_shape=[sds((rows, DI)), sds((DI, N)), sds((rows, 2 * N))],
        scratch_shapes=[pltpu.VMEM((rows, rows), F32)],
        name="scan_fwd",
    )(conv_in, conv_in, halo, halo, taps, taps, bias, bias, col, row, skip)


def gate_fwd(y, gate, incoming, bc, col, gain):
    rows = y.shape[0]
    return pl.pallas_call(
        gate_fwd_kernel,
        grid=(G,),
        in_specs=[col_block(rows), col_block(rows), STATE, fixed((rows, 2 * N)), packs(rows)[0], fixed((1, DI))],
        out_specs=[col_block(rows), fixed((rows, DI))],
        out_shape=[sds((rows, DI)), sds((rows, DI), BF)],
        scratch_shapes=[pltpu.VMEM((G, rows, W), F32), pltpu.VMEM((rows, W), F32)],
        name="gate_fwd",
    )(y, gate, incoming, bc, col, gain)


def gate_bwd(ssm, gate, dn, gain, col, bc):
    rows = ssm.shape[0]
    block = pl.BlockSpec((rows, W), lambda p, g: (0, g))
    late = pl.BlockSpec((rows, W), lambda p, g: (0, p * g))
    return pl.pallas_call(
        gate_bwd_kernel,
        grid=(2, G),
        in_specs=[block, block, block, pl.BlockSpec((1, W), lambda p, g: (0, g)),
                  pl.BlockSpec((1, rows, 2 * K), lambda p, g: (g, 0, 0)),
                  pl.BlockSpec((rows, 2 * N), lambda p, g: (0, 0))],
        out_specs=[late, late, pl.BlockSpec((1, W), lambda p, g: (0, p * g)),
                   pl.BlockSpec((W, N), lambda p, g: (p * g, 0))],
        out_shape=[sds((rows, DI)), sds((rows, DI), BF), sds((1, DI)), sds((DI, N))],
        scratch_shapes=[pltpu.VMEM((rows, W), F32), pltpu.VMEM((rows, W), F32),
                        pltpu.VMEM((rows, 1), F32), pltpu.VMEM((rows, 1), F32)],
        name="gate_bwd",
    )(ssm, gate, dn, gain, col, bc)


def scan_bwd(conv_in, halo, taps, bias, col, row, skip, bc, dy, incoming, outgoing):
    rows = conv_in.shape[0]
    return pl.pallas_call(
        scan_bwd_kernel,
        grid=(G,),
        in_specs=conv_specs(rows) + [fixed((rows, 2 * N)), col_block(rows), STATE, STATE],
        out_specs=[col_block(rows), col_block(8), col_block(8), fixed((rows, W)), fixed((8, W)), fixed((8, W))]
        + packs(rows) + [pl.BlockSpec((1, 8, W), lambda g: (g, 0, 0))],
        out_shape=[sds((rows, DI)), sds((8, DI)), sds((8, DI)), sds((rows, W)), sds((8, W)), sds((8, W)),
                   sds((G, rows, 2 * K)), sds((G, 2 * K, rows)), sds((G, 8, W))],
        scratch_shapes=[pltpu.VMEM((rows, rows), F32), pltpu.VMEM((rows, rows), F32), pltpu.VMEM((rows, 2 * N), F32)],
        name="scan_bwd",
    )(conv_in, conv_in, halo, halo, taps, taps, bias, bias, col, row, skip, bc, dy, incoming, outgoing)


def passed_along(value, axis, steps):
    count = lax.axis_size(axis)
    initial, last = (max(0, -steps), min(count, count - steps))
    return lax.ppermute(value, axis, [(source, source + steps) for source in range(initial, last)])


CHUNKS = 2


def carry(totals, local_state, steps, side=None):
    hops = lax.axis_size("ctx") - 1
    size = DI // CHUNKS
    parts = []
    for chunk in range(CHUNKS):
        rows = slice(chunk * size, chunk * size + size)
        own, factor = local_state[rows], totals[rows]
        incoming = passed_along(own.astype(BF), "ctx", steps)
        for hop in range(hops - 1):
            if side is not None and chunk == 0 and hop == hops - 2:
                incoming, side = lax.optimization_barrier((incoming, side))
            incoming = passed_along((factor * incoming.astype(F32) + own).astype(BF), "ctx", steps)
        parts.append(incoming)
    return jnp.concatenate(parts, 0), side


def all_sum(value):
    for axis in ("fsdp", "ctx"):
        count = lax.axis_size(axis)
        if count & (count - 1):
            value = lax.psum(value, axis)
            continue
        bit = 1
        while bit < count:
            value = value + lax.ppermute(value, axis, [(i, i ^ bit) for i in range(count)])
            bit *= 2
    return value


def rms_norm(values, gain_row):
    return values * lax.rsqrt(jnp.mean(values * values, axis=-1, keepdims=True) + EPS) * gain_row


def rows_product(left, right):
    return lax.dot_general(left, right, (((0,), (0,)), ((), ())), preferred_element_type=F32)


def right_transposed(left, right):
    return lax.dot_general(left, right, (((1,), (1,)), ((), ())), preferred_element_type=F32)


def gathered(value):
    return lax.all_gather(value, "fsdp", axis=0, tiled=True)


def to_owners(split):
    moved = lax.all_to_all(jnp.transpose(split, (1, 0, 2)), "fsdp", split_axis=0, concat_axis=0, tiled=True)
    return moved.reshape(-1, split.shape[2])


def by_run(normed):
    rows, model = normed.shape
    blocks = normed.reshape(rows, lax.axis_size("fsdp"), lax.axis_size("ctx"), -1)
    return jnp.transpose(blocks, (0, 2, 1, 3)).reshape(rows, model)


def run_sum(flat):
    return lax.psum_scatter(flat, "ctx", scatter_dimension=0, tiled=True)


def gate_owners(d_gate):
    return to_owners(d_gate.reshape(d_gate.shape[0], lax.axis_size("fsdp"), -1))


def out_parts(norm_cols, grad_all):
    ctx_count = lax.axis_size("ctx")
    width, model = norm_cols.shape[1], grad_all.shape[1]
    part = rows_product(norm_cols, grad_all).astype(BF)
    part = part.reshape(ctx_count, width // ctx_count, model // width, width)
    return jnp.transpose(part, (0, 2, 1, 3)).reshape(ctx_count, -1, width)


def early_sum(part_gate, part_out, model):
    ctx_count = lax.axis_size("ctx")
    in_rows, width = part_gate.shape[0] // ctx_count, part_gate.shape[1]
    part_gate = part_gate.reshape(ctx_count, in_rows, width)
    summed = run_sum(jnp.concatenate([part_gate, part_out], 1).reshape(-1, width))
    owned_out = jnp.transpose(summed[in_rows:].reshape(model // width, -1, width), (1, 0, 2))
    return summed[:in_rows], owned_out.reshape(-1, model).astype(F32)


def rest_owners(d_rest):
    fsdp_count = lax.axis_size("fsdp")
    rows = d_rest.shape[0]
    wide = d_rest[:, :DI].reshape(rows, fsdp_count, -1)
    narrow = d_rest[:, DI:].reshape(rows, fsdp_count, -1)
    width = wide.shape[2] + narrow.shape[2]
    return to_owners(jnp.concatenate([wide, narrow, jnp.zeros((rows, fsdp_count, -width % 128), BF)], 2))


def rest_parts(normed_all, rest_cols):
    width = (CC - DI + H + DI) // lax.axis_size("fsdp")
    part = rows_product(normed_all, rest_cols)[:, :width].astype(BF)
    return with_layout_constraint(part, Layout(major_to_minor=(0, 1)))


def late_sum(part_rest, gate_sum):
    fsdp_count = lax.axis_size("fsdp")
    width = gate_sum.shape[1]
    both = jnp.concatenate([gate_sum, run_sum(part_rest)], 1)
    both = both.reshape(fsdp_count, -1, both.shape[1])
    both = lax.all_to_all(both, "fsdp", split_axis=0, concat_axis=0, tiled=True)
    both = jnp.transpose(both, (1, 0, 2))
    own = both.shape[0]
    parts = (both[:, :, :width], both[:, :, width : 2 * width], both[:, :, 2 * width :])
    return jnp.concatenate([part.reshape(own, -1) for part in parts], 1).astype(F32)


def grouped(cum, steps):
    rows = cum.shape[0]
    both = jnp.stack([cum.reshape(rows, G, K), steps.reshape(rows, G, K)], 2).reshape(rows, G, 2 * K)
    return jnp.transpose(both, (1, 0, 2)), jnp.transpose(both, (1, 2, 0))


def local(
    activations,
    in_weight,
    out_weight,
    norm_gain,
    conv_weight,
    conv_bias,
    step_bias,
    decay_log,
    skip_gain,
    gate_gain,
    cotangent,
):
    rows = activations.shape[0]
    edge_count = CONV - 1
    order = jnp.arange(rows)
    lower = (order[:, None] >= order[None, :]).astype(F32)
    model = out_weight.shape[2]
    first = gathered(in_weight[0])
    weights = [(first[:, DI:], first[:, :DI], gathered(out_weight[0]))]
    for k in range(1, LAYERS):
        w_conv = gathered(in_weight[k][:, DI:])
        own_out, w_conv = lax.optimization_barrier((out_weight[k], w_conv))
        weights.append((w_conv, gathered(in_weight[k][:, :DI]), gathered(own_out)))
    stream = activations
    kept = []
    for k in range(LAYERS):
        w_conv, w_gate, w_out = weights[k]
        normed = rms_norm(stream, norm_gain[k]).astype(BF)
        proj = jnp.dot(normed, w_conv, preferred_element_type=F32)
        conv_in = proj[:, :CC].astype(BF)
        raw_steps = proj[:, CC:]
        edge_in = passed_along(conv_in[rows - edge_count :], "ctx", 1)
        halo = jnp.concatenate([jnp.zeros((8 - edge_count, CC), F32), edge_in.astype(F32)], 0)
        steps = jax.nn.softplus(raw_steps + step_bias[k][None, :])
        cum = jnp.dot(lower, -steps * jnp.exp(decay_log[k])[None, :], precision=HIGH)
        col, row = grouped(cum, steps)
        totals = jnp.repeat(jnp.exp(cum[-1]), P_SIZE)[:, None]
        skip = jnp.repeat(skip_gain[k], P_SIZE)[None, :]
        bias = conv_bias[k][None, :]
        y, state, bc = scan_fwd(conv_in, halo, conv_weight[k], bias, col, row, skip)
        gate_in = jnp.dot(normed, w_gate, preferred_element_type=F32)
        incoming, _ = carry(totals, state, 1)
        ssm, gnormed = gate_fwd(y, gate_in, incoming, bc, col, gate_gain[k][None, :])
        kept.append((stream, normed, gate_in, conv_in, halo, raw_steps, steps, col, row, totals, skip, bias, bc,
                     incoming, ssm, gnormed))
        stream = stream + jnp.dot(gnormed, w_out, preferred_element_type=F32)
    grad_stream = cotangent
    gnormed_cols = to_owners(kept[-1][-1].reshape(rows, lax.axis_size("fsdp"), -1))
    collected, owned_ins, waiting = [], [], None
    for k in reversed(range(LAYERS)):
        w_conv, w_gate, w_out = weights[k]
        (stream_in, normed, gate_in, conv_in, halo, raw_steps, steps, col, row, totals, skip, bias, bc,
         incoming, ssm, gnormed) = kept[k]
        grad_bf = grad_stream.astype(BF)
        d_gnormed = right_transposed(grad_bf, w_out)
        d_ssm, d_gate, g_gate, local_grad = gate_bwd(ssm, gate_in, d_gnormed, gate_gain[k][None, :], col, bc)
        local_grad, gnormed_cols = lax.optimization_barrier((local_grad, gnormed_cols))
        if waiting is None:
            tokens = gathered(jnp.concatenate([by_run(normed), grad_bf], 1))
            normed_all, grad_all = tokens[:, :model], tokens[:, model:]
        else:
            local_grad, rest_cols = lax.optimization_barrier((local_grad, waiting[1]))
            own_grad, gate_sum = lax.optimization_barrier((grad_bf, waiting[2]))
            normed_all, grad_all = next_normed, gathered(own_grad)
        side = [right_transposed(d_gate, w_gate), gate_owners(d_gate)]
        if waiting is None:
            side.append(stream)
        outgoing, side = carry(totals, local_grad, -1, side)
        d_normed, gate_cols = side[:2]
        if waiting is None:
            stream = side[2]
        if k:
            own_normed, grad_all = lax.optimization_barrier((by_run(kept[k - 1][1]), grad_all))
            next_normed = gathered(own_normed)
        part_gate = rows_product(normed_all, gate_cols).astype(BF)
        part_out = out_parts(gnormed_cols, grad_all)
        if waiting is None:
            outgoing, part_gate, part_out = lax.optimization_barrier((outgoing, part_gate, part_out))
        else:
            part_rest = rest_parts(waiting[0], rest_cols)
            outgoing, part_gate, part_out, part_rest = lax.optimization_barrier(
                (outgoing, part_gate, part_out, part_rest))
            owned_ins.append(late_sum(part_rest, gate_sum))
        if k:
            outgoing, next_gnormed = lax.optimization_barrier((outgoing, kept[k - 1][-1]))
            gnormed_cols = to_owners(next_gnormed.reshape(rows, lax.axis_size("fsdp"), -1))
        gate_sum, owned_out = early_sum(part_gate, part_out, model)
        d_x, edge_x, gt_x, d_bc, edge_bc, gt_bc, colo, rowo, misc = scan_bwd(
            conv_in, halo, conv_weight[k], bias, col, row, skip, bc, d_ssm, incoming, outgoing)
        if k:
            d_x, gnormed_cols = lax.optimization_barrier((d_x, gnormed_cols))
        edges = jnp.concatenate([edge_x[:edge_count], edge_bc[:edge_count]], 1)
        edge_back = passed_along(edges, "ctx", -1)
        taps_grad = jnp.concatenate([gt_x, gt_bc], 1)
        colf = jnp.transpose(colo, (1, 0, 2))
        d_cum = colf[:, :, :K].reshape(rows, H) - jnp.transpose(rowo[:, :K], (2, 0, 1)).reshape(rows, H)
        g_skip = misc[:, 0].reshape(H, P_SIZE).sum(1)
        r_sum = misc[:, 1].reshape(H, P_SIZE).sum(1)
        hg = jnp.transpose(misc[:, 2:4].reshape(G, 2, 2, N), (0, 2, 1, 3)).sum(-1).reshape(H)
        d_last = r_sum + totals[::P_SIZE, 0] * hg
        d_cum = d_cum + jnp.where(order[:, None] == rows - 1, d_last[None, :], 0.0)
        d_log = jnp.dot(lower.T, d_cum, precision=HIGH)
        rate = jnp.exp(decay_log[k])[None, :]
        d_step = colf[:, :, K:].reshape(rows, H) - d_log * rate
        d_raw = d_step * jax.nn.sigmoid(raw_steps + step_bias[k][None, :])
        g_bias = d_raw.sum(0)
        g_log = -(d_log * steps * rate).sum(0)
        d_conv = jnp.concatenate([d_x, d_bc], 1)
        d_conv = d_conv + jnp.pad(edge_back, ((rows - edge_count, 0), (0, 0)))
        d_rest = jnp.concatenate([d_conv, d_raw], 1).astype(BF)
        d_normed = d_normed + right_transposed(d_rest, w_conv)
        _, pullback = jax.vjp(rms_norm, stream_in, norm_gain[k])
        d_stream, g_norm = pullback(d_normed)
        grad_stream = grad_stream + d_stream
        waiting = (normed_all, rest_owners(d_rest), gate_sum)
        small = [g_norm, taps_grad[:CONV].reshape(-1), taps_grad[CONV], g_bias, g_log, g_skip, g_gate.reshape(-1)]
        collected.append((owned_out, small))
    sizes = [part.shape[0] for part in collected[0][1]]
    flat = jnp.concatenate([part for entry in collected[::-1] for part in entry[1]])
    flat = jnp.pad(flat, (0, -flat.shape[0] % 1024)).reshape(-1, 128)
    flat, part_rest = lax.optimization_barrier((flat, rest_parts(waiting[0], waiting[1])))
    owned_ins.append(late_sum(part_rest, waiting[2]))
    flat = all_sum(flat).reshape(-1)[: LAYERS * sum(sizes)].reshape(LAYERS, -1)
    stacked = [jnp.stack(owned_ins[::-1], 0), jnp.stack([entry[0] for entry in collected[::-1]], 0)]
    at = 0
    for size in sizes:
        stacked.append(flat[:, at : at + size])
        at += size
    stacked[3] = stacked[3].reshape(LAYERS, CONV, CC)
    return (stream, grad_stream, *stacked)


def solution(mesh):
    tokens = P(("fsdp", "ctx"), None)
    sharded = P(None, "fsdp", None)
    owned = P(None, ("fsdp", "ctx"), None)
    return jax.shard_map(
        local,
        mesh=mesh,
        in_specs=(tokens, sharded, sharded) + (P(),) * 7 + (tokens,),
        out_specs=(tokens, tokens, owned, owned) + (P(),) * 7,
        check_vma=False,
    )
```

```python
import jax
import jax.numpy as jnp
from jax import lax
from jax.experimental import pallas as pl
from jax.experimental.layout import Layout, with_layout_constraint
from jax.experimental.pallas import tpu as pltpu
from jax.sharding import PartitionSpec as P


H = 48
P_SIZE = 64
N = 128
CONV = 4
LAYERS = 2
DI = 3072
CC = 3328
W = 256
G = DI // W
K = W // P_SIZE

EPS = 1e-05
HIGH = lax.Precision.HIGHEST
F32 = jnp.float32
BF = jnp.bfloat16


def mm(a, b):
    return lax.dot_general(a.astype(BF), b.astype(BF), (((1,), (0,)), ((), ())), preferred_element_type=F32)


def mm_nt(a, b):
    return lax.dot_general(a.astype(BF), b.astype(BF), (((1,), (1,)), ((), ())), preferred_element_type=F32)


def mm_tn(a, b):
    return lax.dot_general(a.astype(BF), b.astype(BF), (((0,), (0,)), ((), ())), preferred_element_type=F32)


def extend(halo_ref, conv_ref):
    return jnp.concatenate([halo_ref[...], conv_ref[...].astype(F32)], 0)


def conv_pre(ext, taps_ref, bias_ref, rows):
    acc = bias_ref[...] + ext[5 : 5 + rows] * taps_ref[0:1, :]
    for j in range(1, CONV):
        acc = acc + ext[5 + j : 5 + j + rows] * taps_ref[j : j + 1, :]
    return acc


def sigmoid(v):
    return 1.0 / (1.0 + jnp.exp(-v))


def pair_cols(col, first, low):
    return jnp.where(low, col[:, first : first + 1], col[:, first + 1 : first + 2])


def masked_scores(c_rows, b_rows):
    s = mm_nt(c_rows, b_rows)
    r = lax.broadcasted_iota(jnp.int32, s.shape, 0)
    q = lax.broadcasted_iota(jnp.int32, s.shape, 1)
    return jnp.where(r >= q, s, 0.0)


def scan_fwd_kernel(conv_ref, conv_bc_ref, halo_ref, halo_bc_ref, taps_ref, taps_bc_ref, bias_ref, bias_bc_ref,
                    col_ref, row_ref, skip_ref, y_ref, state_ref, bc_ref, s_ref):
    rows = conv_ref.shape[0]

    @pl.when(pl.program_id(0) == 0)
    def _():
        pre = conv_pre(extend(halo_bc_ref, conv_bc_ref), taps_bc_ref, bias_bc_ref, rows)
        bc = pre * sigmoid(pre)
        bc_ref[...] = bc
        s_ref[...] = masked_scores(bc[:, N:], bc[:, :N])

    pre = conv_pre(extend(halo_ref, conv_ref), taps_ref, bias_ref, rows)
    x = pre * sigmoid(pre)
    low = lax.broadcasted_iota(jnp.int32, (rows, 2 * P_SIZE), 1) < P_SIZE
    col = col_ref[0]
    row = row_ref[0]
    b_bf = bc_ref[:, :N].astype(BF)
    for pair in range(K // 2):
        h0 = 2 * pair
        cols = slice(pair * 128, pair * 128 + 128)
        x2 = x[:, cols]
        xs = x2 * pair_cols(col, K + h0, low)
        mixes, parts = [], []
        for i in range(2):
            h = h0 + i
            decay = jnp.exp(jnp.minimum(col[:, h : h + 1] - row[h : h + 1, :], 0.0))
            mixes.append((s_ref[...] * decay).astype(BF))
            parts.append(jnp.where(low if i == 0 else ~low, xs, 0.0).astype(BF))
        y = mm(jnp.concatenate(mixes, 1), jnp.concatenate(parts, 0))
        y_ref[:, cols] = y + skip_ref[:, cols] * x2
        last = jnp.where(low[:1], row[h0 : h0 + 1, rows - 1 : rows], row[h0 + 1 : h0 + 2, rows - 1 : rows])
        tail = jnp.exp(last - pair_cols(col, h0, low))
        state_ref[cols, :] = mm_tn(xs * tail, b_bf)


def gate_fwd_kernel(y_ref, gate_ref, in_ref, bc_ref, col_ref, gain_ref, ssm_ref, gn_ref, gated_ref, acc_ref):
    g = pl.program_id(0)
    rows = y_ref.shape[0]

    @pl.when(g == 0)
    def _():
        acc_ref[...] = jnp.zeros_like(acc_ref)

    low = lax.broadcasted_iota(jnp.int32, (rows, 2 * P_SIZE), 1) < P_SIZE
    col = col_ref[0]
    z = mm_nt(bc_ref[:, N:], in_ref[...])
    e = jnp.concatenate([jnp.exp(pair_cols(col, 2 * p, low)) for p in range(K // 2)], 1)
    ssm = y_ref[...] + e * z
    ssm_ref[...] = ssm
    gate = gate_ref[...]
    gated = ssm * (gate * sigmoid(gate))
    gated_ref[g] = gated
    acc_ref[...] += gated * gated

    @pl.when(g == G - 1)
    def _():
        r = lax.rsqrt(jnp.sum(acc_ref[...], 1, keepdims=True) / DI + EPS)
        for i in range(G):
            cols = slice(i * W, i * W + W)
            gn_ref[:, cols] = (gated_ref[i] * r * gain_ref[:, cols]).astype(BF)


def gate_bwd_kernel(ssm_ref, gate_ref, dn_ref, gain_ref, col_ref, bc_ref, dssm_ref, dgate_ref, ggain_ref, lg_ref,
                    sq_ref, dot_ref, r_ref, k_ref):
    phase = pl.program_id(0)
    g = pl.program_id(1)
    rows = ssm_ref.shape[0]
    ssm = ssm_ref[...]
    gate = gate_ref[...]
    sig = sigmoid(gate)
    act = gate * sig
    gated = ssm * act
    dn = dn_ref[...]
    dng = dn * gain_ref[...]

    @pl.when((phase == 0) & (g == 0))
    def _():
        sq_ref[...] = jnp.zeros_like(sq_ref)
        dot_ref[...] = jnp.zeros_like(dot_ref)

    @pl.when(phase == 0)
    def _():
        sq_ref[...] += gated * gated
        dot_ref[...] += dng * gated

    @pl.when((phase == 1) & (g == 0))
    def _():
        r = lax.rsqrt(jnp.sum(sq_ref[...], 1, keepdims=True) / DI + EPS)
        r_ref[...] = r
        k_ref[...] = r * r * r * jnp.sum(dot_ref[...], 1, keepdims=True) / DI

    @pl.when(phase == 1)
    def _():
        r = r_ref[...]
        dgated = r * dng - gated * k_ref[...]
        dssm = dgated * act
        dssm_ref[...] = dssm
        dgate_ref[...] = (dgated * ssm * (sig * (1.0 + gate * (1.0 - sig)))).astype(BF)
        ggain_ref[...] = jnp.sum(dn * (gated * r), 0, keepdims=True)
        low = lax.broadcasted_iota(jnp.int32, (rows, 2 * P_SIZE), 1) < P_SIZE
        col = col_ref[0]
        e = jnp.concatenate([jnp.exp(pair_cols(col, 2 * p, low)) for p in range(K // 2)], 1)
        lg_ref[...] = mm_tn(dssm * e, bc_ref[:, N:])


def conv_back(d_act, pre, sig, ext, taps_ref, rows):
    d_pre = d_act * (sig * (1.0 + pre * (1.0 - sig)))
    zero = jnp.zeros((8, d_pre.shape[1]), F32)
    below = jnp.concatenate([d_pre, zero], 0)
    above = jnp.concatenate([zero, d_pre[:8]], 0)
    d_conv = below[3 : 3 + rows] * taps_ref[0:1, :]
    edge = above[8:16] * taps_ref[0:1, :]
    terms = [jnp.sum(d_pre * ext[5 : 5 + rows], 0, keepdims=True)]
    for j in range(1, CONV):
        d_conv = d_conv + below[3 - j : 3 - j + rows] * taps_ref[j : j + 1, :]
        edge = edge + above[8 - j : 16 - j] * taps_ref[j : j + 1, :]
        terms.append(jnp.sum(d_pre * ext[5 + j : 5 + j + rows], 0, keepdims=True))
    terms.append(jnp.sum(d_pre, 0, keepdims=True))
    return d_conv, edge, terms


def scan_bwd_kernel(conv_ref, conv_bc_ref, halo_ref, halo_bc_ref, taps_ref, taps_bc_ref, bias_ref, bias_bc_ref,
                    col_ref, row_ref, skip_ref, bc_ref, dy_ref, in_ref, out_ref,
                    dconv_ref, edge_ref, gt_ref, dconv_bc_ref, edge_bc_ref, gt_bc_ref, colo_ref, rowo_ref, misc_ref,
                    s_ref, ds_ref, dbc_ref):
    g = pl.program_id(0)
    rows = conv_ref.shape[0]

    @pl.when(g == 0)
    def _():
        s_ref[...] = masked_scores(bc_ref[:, N:], bc_ref[:, :N])
        ds_ref[...] = jnp.zeros_like(ds_ref)
        dbc_ref[...] = jnp.zeros_like(dbc_ref)

    ext = extend(halo_ref, conv_ref)
    pre = conv_pre(ext, taps_ref, bias_ref, rows)
    sig = sigmoid(pre)
    x = pre * sig
    low = lax.broadcasted_iota(jnp.int32, (rows, 2 * P_SIZE), 1) < P_SIZE
    lane = lax.broadcasted_iota(jnp.int32, (rows, 2 * K), 1)
    col = col_ref[0]
    row = row_ref[0]
    b_bf = bc_ref[:, :N].astype(BF)
    c_bf = bc_ref[:, N:].astype(BF)
    colo = jnp.zeros((rows, 2 * K), F32)
    dxs = []
    misc_ref[...] = jnp.zeros_like(misc_ref)
    rowo_ref[...] = jnp.zeros_like(rowo_ref)
    for pair in range(K // 2):
        h0 = 2 * pair
        cols = slice(pair * 128, pair * 128 + 128)
        x2 = x[:, cols]
        step = pair_cols(col, K + h0, low)
        xs = x2 * step
        xs_bf = xs.astype(BF)
        dy = dy_ref[:, cols]
        h_in = in_ref[cols, :]
        h_out = out_ref[cols, :]
        cum = pair_cols(col, h0, low)
        e = jnp.exp(cum)
        last = jnp.where(low[:1], row[h0 : h0 + 1, rows - 1 : rows], row[h0 + 1 : h0 + 2, rows - 1 : rows])
        tail = jnp.exp(last - cum)
        edy = e * dy
        txs = tail * xs
        inter = edy * mm_nt(c_bf, h_in)
        u = mm_nt(b_bf, h_out)
        r = txs * u
        dbc_ref[:, N:] += mm(edy, h_in)
        dbc_ref[:, :N] += mm(txs, h_out)
        d_xs = tail * u
        side = inter - r
        for i in range(2):
            h = h0 + i
            keep = low if i == 0 else ~low
            dyh = jnp.where(keep, dy, 0.0).astype(BF)
            d_mix = mm_nt(dyh, xs_bf)
            decay = jnp.exp(jnp.minimum(col[:, h : h + 1] - row[h : h + 1, :], 0.0))
            d_ld = d_mix * decay
            ds_ref[...] += d_ld
            s = s_ref[...]
            weight = d_ld * s
            d_xs = d_xs + mm_tn(s * decay, dyh)
            rowo_ref[0, h : h + 1, :] = jnp.sum(weight, 0, keepdims=True)
            folded = weight[:, :128] + weight[:, 128:] + jnp.where(keep, side, 0.0)
            colo = jnp.where(lane == h, jnp.sum(folded, 1, keepdims=True), colo)
        prod = x2 * d_xs
        for i in range(2):
            keep = low if i == 0 else ~low
            s_sum = jnp.sum(jnp.where(keep, prod, 0.0), 1, keepdims=True)
            colo = jnp.where(lane == K + h0 + i, s_sum, colo)
        dxs.append(step * d_xs + skip_ref[:, cols] * dy)
        hg = h_in.astype(F32) * h_out.astype(F32)
        misc_ref[0, 0:1, cols] = jnp.sum(dy * x2, 0, keepdims=True)
        misc_ref[0, 1:2, cols] = jnp.sum(r, 0, keepdims=True)
        misc_ref[0, 2:3, cols] = jnp.sum(hg[:P_SIZE], 0, keepdims=True)
        misc_ref[0, 3:4, cols] = jnp.sum(hg[P_SIZE:], 0, keepdims=True)
    colo_ref[0] = colo
    d_conv, edge, terms = conv_back(jnp.concatenate(dxs, 1), pre, sig, ext, taps_ref, rows)
    dconv_ref[...] = d_conv
    edge_ref[...] = edge
    gt_ref[...] = jnp.zeros_like(gt_ref)
    for j, term in enumerate(terms):
        gt_ref[j : j + 1, :] = term

    @pl.when(g == G - 1)
    def _():
        r_i = lax.broadcasted_iota(jnp.int32, ds_ref.shape, 0)
        q_i = lax.broadcasted_iota(jnp.int32, ds_ref.shape, 1)
        ds = jnp.where(r_i >= q_i, ds_ref[...], 0.0).astype(BF)
        d_c = dbc_ref[:, N:] + mm(ds, b_bf)
        d_b = dbc_ref[:, :N] + mm_tn(ds, c_bf)
        ext2 = extend(halo_bc_ref, conv_bc_ref)
        pre2 = conv_pre(ext2, taps_bc_ref, bias_bc_ref, rows)
        d_conv2, edge2, terms2 = conv_back(
            jnp.concatenate([d_b, d_c], 1), pre2, sigmoid(pre2), ext2, taps_bc_ref, rows)
        dconv_bc_ref[...] = d_conv2
        edge_bc_ref[...] = edge2
        gt_bc_ref[...] = jnp.zeros_like(gt_bc_ref)
        for j, term in enumerate(terms2):
            gt_bc_ref[j : j + 1, :] = term


def col_block(rows):
    return pl.BlockSpec((rows, W), lambda g: (0, g))


def bc_block(rows):
    return pl.BlockSpec((rows, W), lambda g: (0, G))


def fixed(shape):
    return pl.BlockSpec(shape, lambda g: (0,) * len(shape))


def packs(rows):
    return [pl.BlockSpec((1, rows, 2 * K), lambda g: (g, 0, 0)), pl.BlockSpec((1, 2 * K, rows), lambda g: (g, 0, 0))]


def conv_specs(rows):
    return [col_block(rows), bc_block(rows), col_block(8), bc_block(8), col_block(CONV), bc_block(CONV),
            col_block(1), bc_block(1)] + packs(rows) + [col_block(1)]


STATE = pl.BlockSpec((W, N), lambda g: (g, 0))


def sds(shape, dtype=F32):
    return jax.ShapeDtypeStruct(shape, dtype)


def scan_fwd(conv_in, halo, taps, bias, col, row, skip):
    rows = conv_in.shape[0]
    return pl.pallas_call(
        scan_fwd_kernel,
        grid=(G,),
        in_specs=conv_specs(rows),
        out_specs=[col_block(rows), STATE, fixed((rows, 2 * N))],
        out_shape=[sds((rows, DI)), sds((DI, N)), sds((rows, 2 * N))],
        scratch_shapes=[pltpu.VMEM((rows, rows), F32)],
        name="scan_fwd",
    )(conv_in, conv_in, halo, halo, taps, taps, bias, bias, col, row, skip)


def gate_fwd(y, gate, incoming, bc, col, gain):
    rows = y.shape[0]
    return pl.pallas_call(
        gate_fwd_kernel,
        grid=(G,),
        in_specs=[col_block(rows), col_block(rows), STATE, fixed((rows, 2 * N)), packs(rows)[0], fixed((1, DI))],
        out_specs=[col_block(rows), fixed((rows, DI))],
        out_shape=[sds((rows, DI)), sds((rows, DI), BF)],
        scratch_shapes=[pltpu.VMEM((G, rows, W), F32), pltpu.VMEM((rows, W), F32)],
        name="gate_fwd",
    )(y, gate, incoming, bc, col, gain)


def gate_bwd(ssm, gate, dn, gain, col, bc):
    rows = ssm.shape[0]
    block = pl.BlockSpec((rows, W), lambda p, g: (0, g))
    late = pl.BlockSpec((rows, W), lambda p, g: (0, p * g))
    return pl.pallas_call(
        gate_bwd_kernel,
        grid=(2, G),
        in_specs=[block, block, block, pl.BlockSpec((1, W), lambda p, g: (0, g)),
                  pl.BlockSpec((1, rows, 2 * K), lambda p, g: (g, 0, 0)),
                  pl.BlockSpec((rows, 2 * N), lambda p, g: (0, 0))],
        out_specs=[late, late, pl.BlockSpec((1, W), lambda p, g: (0, p * g)),
                   pl.BlockSpec((W, N), lambda p, g: (p * g, 0))],
        out_shape=[sds((rows, DI)), sds((rows, DI), BF), sds((1, DI)), sds((DI, N))],
        scratch_shapes=[pltpu.VMEM((rows, W), F32), pltpu.VMEM((rows, W), F32),
                        pltpu.VMEM((rows, 1), F32), pltpu.VMEM((rows, 1), F32)],
        name="gate_bwd",
    )(ssm, gate, dn, gain, col, bc)


def scan_bwd(conv_in, halo, taps, bias, col, row, skip, bc, dy, incoming, outgoing):
    rows = conv_in.shape[0]
    return pl.pallas_call(
        scan_bwd_kernel,
        grid=(G,),
        in_specs=conv_specs(rows) + [fixed((rows, 2 * N)), col_block(rows), STATE, STATE],
        out_specs=[col_block(rows), col_block(8), col_block(8), fixed((rows, W)), fixed((8, W)), fixed((8, W))]
        + packs(rows) + [pl.BlockSpec((1, 8, W), lambda g: (g, 0, 0))],
        out_shape=[sds((rows, DI)), sds((8, DI)), sds((8, DI)), sds((rows, W)), sds((8, W)), sds((8, W)),
                   sds((G, rows, 2 * K)), sds((G, 2 * K, rows)), sds((G, 8, W))],
        scratch_shapes=[pltpu.VMEM((rows, rows), F32), pltpu.VMEM((rows, rows), F32), pltpu.VMEM((rows, 2 * N), F32)],
        name="scan_bwd",
    )(conv_in, conv_in, halo, halo, taps, taps, bias, bias, col, row, skip, bc, dy, incoming, outgoing)


def passed_along(value, axis, steps):
    count = lax.axis_size(axis)
    initial, last = (max(0, -steps), min(count, count - steps))
    return lax.ppermute(value, axis, [(source, source + steps) for source in range(initial, last)])


CHUNKS = 2


def carry(totals, local_state, steps, side=None):
    hops = lax.axis_size("ctx") - 1
    size = DI // CHUNKS
    parts = []
    for chunk in range(CHUNKS):
        rows = slice(chunk * size, chunk * size + size)
        own, factor = local_state[rows], totals[rows]
        incoming = passed_along(own.astype(BF), "ctx", steps)
        for hop in range(hops - 1):
            if side is not None and hop == hops - 2:
                incoming, done = lax.optimization_barrier((incoming, side[chunk]))
                side = side[:chunk] + [done] + side[chunk + 1 :]
            incoming = passed_along((factor * incoming.astype(F32) + own).astype(BF), "ctx", steps)
        parts.append(incoming)
    return jnp.concatenate(parts, 0), side


def all_sum(value):
    for axis in ("fsdp", "ctx"):
        count = lax.axis_size(axis)
        if count & (count - 1):
            value = lax.psum(value, axis)
            continue
        bit = 1
        while bit < count:
            value = value + lax.ppermute(value, axis, [(i, i ^ bit) for i in range(count)])
            bit *= 2
    return value


def rms_norm(values, gain_row):
    return values * lax.rsqrt(jnp.mean(values * values, axis=-1, keepdims=True) + EPS) * gain_row


def rows_product(left, right):
    return lax.dot_general(left, right, (((0,), (0,)), ((), ())), preferred_element_type=F32)


def right_transposed(left, right):
    return lax.dot_general(left, right, (((1,), (1,)), ((), ())), preferred_element_type=F32)


def gathered(value):
    return lax.all_gather(value, "fsdp", axis=0, tiled=True)


def to_owners(split):
    moved = lax.all_to_all(jnp.transpose(split, (1, 0, 2)), "fsdp", split_axis=0, concat_axis=0, tiled=True)
    return moved.reshape(-1, split.shape[2])


def by_run(normed):
    rows, model = normed.shape
    blocks = normed.reshape(rows, lax.axis_size("fsdp"), lax.axis_size("ctx"), -1)
    return jnp.transpose(blocks, (0, 2, 1, 3)).reshape(rows, model)


def run_sum(flat):
    return lax.psum_scatter(flat, "ctx", scatter_dimension=0, tiled=True)


def gate_owners(d_gate):
    return to_owners(d_gate.reshape(d_gate.shape[0], lax.axis_size("fsdp"), -1))


def out_parts(norm_cols, grad_all):
    ctx_count = lax.axis_size("ctx")
    width, model = norm_cols.shape[1], grad_all.shape[1]
    part = rows_product(norm_cols, grad_all).astype(BF)
    part = part.reshape(ctx_count, width // ctx_count, model // width, width)
    return jnp.transpose(part, (0, 2, 1, 3)).reshape(ctx_count, -1, width)


def early_sum(part_gate, part_out, model):
    ctx_count = lax.axis_size("ctx")
    in_rows, width = part_gate.shape[0] // ctx_count, part_gate.shape[1]
    part_gate = part_gate.reshape(ctx_count, in_rows, width)
    summed = run_sum(jnp.concatenate([part_gate, part_out], 1).reshape(-1, width))
    owned_out = jnp.transpose(summed[in_rows:].reshape(model // width, -1, width), (1, 0, 2))
    return summed[:in_rows], owned_out.reshape(-1, model).astype(F32)


def rest_owners(d_rest):
    fsdp_count = lax.axis_size("fsdp")
    rows = d_rest.shape[0]
    wide = d_rest[:, :DI].reshape(rows, fsdp_count, -1)
    narrow = d_rest[:, DI:].reshape(rows, fsdp_count, -1)
    width = wide.shape[2] + narrow.shape[2]
    return to_owners(jnp.concatenate([wide, narrow, jnp.zeros((rows, fsdp_count, -width % 128), BF)], 2))


def rest_parts(normed_all, rest_cols):
    width = (CC - DI + H + DI) // lax.axis_size("fsdp")
    part = rows_product(normed_all, rest_cols)[:, :width].astype(BF)
    return with_layout_constraint(part, Layout(major_to_minor=(0, 1)))


def late_sum(part_rest, gate_sum):
    fsdp_count = lax.axis_size("fsdp")
    width = gate_sum.shape[1]
    both = jnp.concatenate([gate_sum, run_sum(part_rest)], 1)
    both = both.reshape(fsdp_count, -1, both.shape[1])
    both = lax.all_to_all(both, "fsdp", split_axis=0, concat_axis=0, tiled=True)
    both = jnp.transpose(both, (1, 0, 2))
    own = both.shape[0]
    parts = (both[:, :, :width], both[:, :, width : 2 * width], both[:, :, 2 * width :])
    return jnp.concatenate([part.reshape(own, -1) for part in parts], 1).astype(F32)


def grouped(cum, steps):
    rows = cum.shape[0]
    both = jnp.stack([cum.reshape(rows, G, K), steps.reshape(rows, G, K)], 2).reshape(rows, G, 2 * K)
    return jnp.transpose(both, (1, 0, 2)), jnp.transpose(both, (1, 2, 0))


def local(
    activations,
    in_weight,
    out_weight,
    norm_gain,
    conv_weight,
    conv_bias,
    step_bias,
    decay_log,
    skip_gain,
    gate_gain,
    cotangent,
):
    rows = activations.shape[0]
    edge_count = CONV - 1
    order = jnp.arange(rows)
    lower = (order[:, None] >= order[None, :]).astype(F32)
    model = out_weight.shape[2]
    first = gathered(in_weight[0])
    weights = [(first[:, DI:], first[:, :DI], gathered(out_weight[0]))]
    for k in range(1, LAYERS):
        weights.append((gathered(in_weight[k][:, DI:]), gathered(in_weight[k][:, :DI]), gathered(out_weight[k])))
    stream = activations
    kept = []
    for k in range(LAYERS):
        w_conv, w_gate, w_out = weights[k]
        normed = rms_norm(stream, norm_gain[k]).astype(BF)
        proj = jnp.dot(normed, w_conv, preferred_element_type=F32)
        conv_in = proj[:, :CC].astype(BF)
        raw_steps = proj[:, CC:]
        edge_in = passed_along(conv_in[rows - edge_count :], "ctx", 1)
        halo = jnp.concatenate([jnp.zeros((8 - edge_count, CC), F32), edge_in.astype(F32)], 0)
        steps = jax.nn.softplus(raw_steps + step_bias[k][None, :])
        cum = jnp.dot(lower, -steps * jnp.exp(decay_log[k])[None, :], precision=HIGH)
        col, row = grouped(cum, steps)
        totals = jnp.repeat(jnp.exp(cum[-1]), P_SIZE)[:, None]
        skip = jnp.repeat(skip_gain[k], P_SIZE)[None, :]
        bias = conv_bias[k][None, :]
        y, state, bc = scan_fwd(conv_in, halo, conv_weight[k], bias, col, row, skip)
        gate_in = jnp.dot(normed, w_gate, preferred_element_type=F32)
        incoming, _ = carry(totals, state, 1)
        ssm, gnormed = gate_fwd(y, gate_in, incoming, bc, col, gate_gain[k][None, :])
        kept.append((stream, normed, gate_in, conv_in, halo, raw_steps, steps, col, row, totals, skip, bias, bc,
                     incoming, ssm, gnormed))
        stream = stream + jnp.dot(gnormed, w_out, preferred_element_type=F32)
    grad_stream = cotangent
    gnormed_cols = to_owners(kept[-1][-1].reshape(rows, lax.axis_size("fsdp"), -1))
    collected, owned_ins, waiting = [], [], None
    for k in reversed(range(LAYERS)):
        w_conv, w_gate, w_out = weights[k]
        (stream_in, normed, gate_in, conv_in, halo, raw_steps, steps, col, row, totals, skip, bias, bc,
         incoming, ssm, gnormed) = kept[k]
        grad_bf = grad_stream.astype(BF)
        if waiting is None:
            normed_all, grad_all = gathered(by_run(normed)), gathered(grad_bf)
        else:
            normed_all = next_normed
        if k:
            next_normed = gathered(by_run(kept[k - 1][1]))
        d_gnormed = right_transposed(grad_bf, w_out)
        d_ssm, d_gate, g_gate, local_grad = gate_bwd(ssm, gate_in, d_gnormed, gate_gain[k][None, :], col, bc)
        local_grad, gnormed_cols = lax.optimization_barrier((local_grad, gnormed_cols))
        side = [[right_transposed(d_gate, w_gate), gate_owners(d_gate)]]
        if waiting is None:
            side[0].append(stream)
            side.append([rows_product(normed_all, side[0][1]).astype(BF), out_parts(gnormed_cols, grad_all)])
        else:
            local_grad, rest_cols = lax.optimization_barrier((local_grad, waiting[1]))
            own_grad, gate_sum = lax.optimization_barrier((grad_bf, waiting[2]))
            grad_all = gathered(own_grad)
            side.append([rows_product(normed_all, side[0][1]).astype(BF), rest_parts(waiting[0], rest_cols)])
        outgoing, side = carry(totals, local_grad, -1, side)
        d_normed, part_gate = side[0][0], side[1][0]
        if waiting is None:
            stream, part_out = side[0][2], side[1][1]
        else:
            outgoing, part_out = lax.optimization_barrier((outgoing, out_parts(gnormed_cols, grad_all)))
            owned_ins.append(late_sum(side[1][1], gate_sum))
        if k:
            outgoing, next_gnormed = lax.optimization_barrier((outgoing, kept[k - 1][-1]))
            gnormed_cols = to_owners(next_gnormed.reshape(rows, lax.axis_size("fsdp"), -1))
        gate_sum, owned_out = early_sum(part_gate, part_out, model)
        d_x, edge_x, gt_x, d_bc, edge_bc, gt_bc, colo, rowo, misc = scan_bwd(
            conv_in, halo, conv_weight[k], bias, col, row, skip, bc, d_ssm, incoming, outgoing)
        if k:
            d_x, gnormed_cols = lax.optimization_barrier((d_x, gnormed_cols))
        edges = jnp.concatenate([edge_x[:edge_count], edge_bc[:edge_count]], 1)
        edge_back = passed_along(edges, "ctx", -1)
        taps_grad = jnp.concatenate([gt_x, gt_bc], 1)
        colf = jnp.transpose(colo, (1, 0, 2))
        d_cum = colf[:, :, :K].reshape(rows, H) - jnp.transpose(rowo[:, :K], (2, 0, 1)).reshape(rows, H)
        g_skip = misc[:, 0].reshape(H, P_SIZE).sum(1)
        r_sum = misc[:, 1].reshape(H, P_SIZE).sum(1)
        hg = jnp.transpose(misc[:, 2:4].reshape(G, 2, 2, N), (0, 2, 1, 3)).sum(-1).reshape(H)
        d_last = r_sum + totals[::P_SIZE, 0] * hg
        d_cum = d_cum + jnp.where(order[:, None] == rows - 1, d_last[None, :], 0.0)
        d_log = jnp.dot(lower.T, d_cum, precision=HIGH)
        rate = jnp.exp(decay_log[k])[None, :]
        d_step = colf[:, :, K:].reshape(rows, H) - d_log * rate
        d_raw = d_step * jax.nn.sigmoid(raw_steps + step_bias[k][None, :])
        g_bias = d_raw.sum(0)
        g_log = -(d_log * steps * rate).sum(0)
        d_conv = jnp.concatenate([d_x, d_bc], 1)
        d_conv = d_conv + jnp.pad(edge_back, ((rows - edge_count, 0), (0, 0)))
        d_rest = jnp.concatenate([d_conv, d_raw], 1).astype(BF)
        d_normed = d_normed + right_transposed(d_rest, w_conv)
        _, pullback = jax.vjp(rms_norm, stream_in, norm_gain[k])
        d_stream, g_norm = pullback(d_normed)
        grad_stream = grad_stream + d_stream
        waiting = (normed_all, rest_owners(d_rest), gate_sum)
        small = [g_norm, taps_grad[:CONV].reshape(-1), taps_grad[CONV], g_bias, g_log, g_skip, g_gate.reshape(-1)]
        collected.append((owned_out, small))
    sizes = [part.shape[0] for part in collected[0][1]]
    flat = jnp.concatenate([part for entry in collected[::-1] for part in entry[1]])
    flat = jnp.pad(flat, (0, -flat.shape[0] % 1024)).reshape(-1, 128)
    flat, part_rest = lax.optimization_barrier((flat, rest_parts(waiting[0], waiting[1])))
    owned_ins.append(late_sum(part_rest, waiting[2]))
    flat = all_sum(flat).reshape(-1)[: LAYERS * sum(sizes)].reshape(LAYERS, -1)
    stacked = [jnp.stack(owned_ins[::-1], 0), jnp.stack([entry[0] for entry in collected[::-1]], 0)]
    at = 0
    for size in sizes:
        stacked.append(flat[:, at : at + size])
        at += size
    stacked[3] = stacked[3].reshape(LAYERS, CONV, CC)
    return (stream, grad_stream, *stacked)


def solution(mesh):
    tokens = P(("fsdp", "ctx"), None)
    sharded = P(None, "fsdp", None)
    owned = P(None, ("fsdp", "ctx"), None)
    return jax.shard_map(
        local,
        mesh=mesh,
        in_specs=(tokens, sharded, sharded) + (P(),) * 7 + (tokens,),
        out_specs=(tokens, tokens, owned, owned) + (P(),) * 7,
        check_vma=False,
    )
```
